256 devices in a mesh: hid: 32 (over x, z), tok: 8 (over y, core).
Axes of the slice: x: 4, y: 4, z: 8, core: 2. Of those that a mesh axis runs over, the one named last changes fastest.
Arguments:
- tokens: bfloat16 [2048, 12288], P('tok', 'hid'), may hold values from -6 to 6
- cotangent: bfloat16 [2048, 12288], P('tok', 'hid'), may hold values from -0.75 to 0.75
- up_tiles: bfloat16 [6, 256, 24576], P(None, None, 'hid'), may hold values from -0.15625 to 0.15625
- down_tiles: bfloat16 [6, 24576, 256], P(None, 'hid'), may hold values from -0.109375 to 0.109375
- block_index: int32 [6, 96, 2], P(None, 'hid'), may hold values from 0 to 2, as said below
- up_left: bfloat16 [12288, 256], P('hid'), may hold values from -0.0546875 to 0.0546875
- up_right: bfloat16 [256, 24576], P(None, 'hid'), may hold values from -0.375 to 0.375
- down_left: bfloat16 [24576, 256], P('hid'), may hold values from -0.0390625 to 0.0390625
- down_right: bfloat16 [256, 12288], P(None, 'hid'), may hold values from -0.375 to 0.375
Outputs:
- layer_out: bfloat16 [2048, 12288], P('tok', 'hid')
- grad_tokens: bfloat16 [2048, 12288], P('tok', 'hid')
- grad_up_tiles: bfloat16 [6, 256, 24576], P(None, 'tok', 'hid')
- grad_down_tiles: bfloat16 [6, 24576, 256], P(None, ('hid', 'tok'))
- grad_up_left: bfloat16 [12288, 256], P(('hid', 'tok'))
- grad_up_right: bfloat16 [256, 24576], P('tok', 'hid')
- grad_down_left: bfloat16 [24576, 256], P(('hid', 'tok'))
- grad_down_right: bfloat16 [256, 12288], P('tok', 'hid')
The draws below stay inside these ranges and needn't reach their ends.
Inputs may be any that keep to these rules, and one draw needn't show every extreme that they name: `block_index`: each row names two different sub-blocks.
All inputs are finite; a program needn't handle non-finite values.
Results may differ from the reference program's by a relative error of at most 0.03.
Values may be sent and summed in bfloat16 or wider, within the bound.
No kernel may reach another device: no remote copies, remote signals or barrier semaphores. Data moves between devices by JAX's collectives and lax.ppermute only.
A program may use at most 128 MiB of HBM per device.

```python
import jax
import jax.numpy as jnp
from jax import lax

D = 12288
FF = 24576
HB = 256
RANK = 256
TOK_DEV = 256
LEVELS = 6
SUB = 128
NB = 3
FF_BLOCKS = 96
TOKENS = 2048
N_HID = 32
N_TOK = 8


def draw_block_index(key, part):
    first_key = jax.random.fold_in(key, 11)
    second_key = jax.random.fold_in(key, 23)
    excluded = jax.random.randint(first_key, (LEVELS, FF_BLOCKS), 0, 3, dtype=jnp.int32)
    flipped = jax.random.randint(second_key, (LEVELS, FF_BLOCKS), 0, 2, dtype=jnp.int32)
    leading = (excluded + 1 + flipped) % 3
    trailing_axes = (excluded + 2 - flipped) % 3
    return jnp.stack([leading, trailing_axes], axis=-1).astype(jnp.int32)


def block_levels(own_key, dims, shards, low, top_value):
    loudness, own = 1.0, jax.random.fold_in(own_key, 6)
    for dim, parts in shards:
        steps = jnp.exp(jax.random.uniform(jax.random.fold_in(own, dim), (parts,), jnp.float32, low / len(shards), top_value / len(shards)))
        loudness = loudness * jnp.repeat(steps, dims[dim] // parts).reshape([-1 if axis == dim else 1 for axis in range(len(dims))])
    return loudness


def centred(key, extent, scale, limit, pieces=(), kind=jnp.bfloat16):
    drawn = jax.random.normal(key, extent, jnp.float32) * scale
    if len(pieces) > 0:
        drawn = block_levels(key, extent, pieces, -0.22, 0.18) * drawn
    return jnp.clip(drawn, min=-limit, max=limit).astype(kind)


def setup_inputs(seed: int = 0) -> dict:
    arg_keys = jax.random.split(jax.random.key(seed), 10)
    return {
        "tokens": centred(arg_keys[0], (TOKENS, D), 1.0, 6.0, ((0, 8), (1, 32))),
        "cotangent": centred(arg_keys[1], (TOKENS, D), 0.125, 0.75, ((0, 8), (1, 32))),
        "up_tiles": centred(arg_keys[2], (LEVELS, 2 * SUB, FF), (LEVELS * 2 * SUB) ** -0.5, 0.15625, ((2, 32),)),
        "down_tiles": centred(arg_keys[3], (LEVELS, FF, 2 * SUB), (LEVELS * (FF // N_HID) * 2 // 3) ** -0.5, 0.109375, ((1, 32),)),
        "block_index": draw_block_index(jax.random.fold_in(arg_keys[9], 71), 0),
        "up_left": centred(arg_keys[5], (D, RANK), D ** -0.5, 0.0546875, ((0, 32),)),
        "up_right": centred(arg_keys[6], (RANK, FF), RANK ** -0.5, 0.375, ((1, 32),)),
        "down_left": centred(arg_keys[7], (FF, RANK), FF ** -0.5, 0.0390625, ((0, 32),)),
        "down_right": centred(arg_keys[8], (RANK, D), RANK ** -0.5, 0.375, ((1, 32),)),
    }


GELU_SCALE = 0.7978845608028654
GELU_CUBIC = 0.044715


def gelu_parts(pre_act):
    inner = GELU_SCALE * (pre_act + GELU_CUBIC * pre_act * pre_act * pre_act)
    tanh_value = jnp.tanh(inner)
    value = 0.5 * pre_act * (1.0 + tanh_value)
    slope = 0.5 * (1.0 + tanh_value) + 0.5 * pre_act * (1.0 - tanh_value * tanh_value) * GELU_SCALE * (1.0 + 3.0 * GELU_CUBIC * pre_act * pre_act)
    return value, slope


def partner_list(butterfly_level_index):
    devices = jnp.arange(N_HID, dtype=jnp.int32)
    if butterfly_level_index == 0:
        return devices
    return jnp.bitwise_xor(devices, jnp.int32(1 << (butterfly_level_index - 1)))


def round_groups(partials):
    rounded = lax.optimization_barrier(partials.astype(jnp.bfloat16))
    return jnp.sum(rounded.astype(jnp.float32), axis=0).astype(jnp.bfloat16)


def reference(tokens, cotangent, up_tiles, down_tiles, block_index, up_left, up_right, down_left, down_right):
    features = tokens.reshape(TOKENS, N_HID, 3, SUB)
    grad_fields = cotangent.reshape(TOKENS, N_HID, 3, SUB)
    index_all = block_index.reshape(LEVELS, N_HID, NB, 2)
    device_grid = jnp.broadcast_to(jnp.arange(N_HID, dtype=jnp.int32)[:, None, None], (N_HID, NB, 2))
    selectors = (index_all[..., None] == jnp.arange(3, dtype=jnp.int32)).astype(jnp.float32)

    def select_blocks(field, butterfly_level_index):
        moved = field[:, partner_list(butterfly_level_index)]
        return moved[:, device_grid, index_all[butterfly_level_index]]

    def place_blocks(partner_pairs, butterfly_level_index):
        placed_blocks = jnp.einsum("tpbjs,pbjc->tpcs", partner_pairs, selectors[butterfly_level_index], precision=lax.Precision.HIGHEST)
        rounded = placed_blocks.astype(jnp.bfloat16)
        return rounded[:, partner_list(butterfly_level_index)].astype(jnp.float32)

    pre_act = jnp.zeros((TOKENS, N_HID, NB, HB), jnp.float32)
    for partition_key in range(LEVELS):
        chosen = select_blocks(features, partition_key).astype(jnp.float32)
        weights_level = up_tiles[partition_key].reshape(2, SUB, N_HID, NB, HB).astype(jnp.float32)
        pre_act = pre_act + jnp.einsum("tpbjs,jspbh->tpbh", chosen, weights_level)
    low_up = jnp.dot(tokens, up_left, preferred_element_type=jnp.float32).astype(jnp.bfloat16)
    pre_act = pre_act + jnp.dot(low_up, up_right, preferred_element_type=jnp.float32).reshape(TOKENS, N_HID, NB, HB)
    hidden_value, slope = gelu_parts(pre_act)
    hidden_act = hidden_value.astype(jnp.bfloat16)
    hidden_flat = hidden_act.reshape(TOKENS, FF)
    low_down = jnp.dot(hidden_flat, down_left, preferred_element_type=jnp.float32).astype(jnp.bfloat16)
    output_acc = jnp.zeros((TOKENS, N_HID, 3, SUB), jnp.float32)
    for partition_key in range(LEVELS):
        weights_level = down_tiles[partition_key].reshape(N_HID, NB, HB, 2, SUB).astype(jnp.float32)
        partner_pairs = jnp.einsum("tpbh,pbhjs->tpbjs", hidden_act.astype(jnp.float32), weights_level)
        output_acc = output_acc + place_blocks(partner_pairs, partition_key)
    layer_out = (output_acc.reshape(TOKENS, D) + jnp.dot(low_down, down_right, preferred_element_type=jnp.float32)).astype(jnp.bfloat16)

    back_down = jnp.dot(cotangent, down_right.T, preferred_element_type=jnp.float32).astype(jnp.bfloat16)
    grad_hidden = jnp.dot(back_down, down_left.T, preferred_element_type=jnp.float32).reshape(TOKENS, N_HID, NB, HB)
    hidden_groups = hidden_act.astype(jnp.float32).reshape(N_TOK, TOK_DEV, N_HID, NB, HB)
    down_list = []
    for partition_key in range(LEVELS):
        chosen = select_blocks(grad_fields, partition_key).astype(jnp.float32)
        weights_level = down_tiles[partition_key].reshape(N_HID, NB, HB, 2, SUB).astype(jnp.float32)
        grad_hidden = grad_hidden + jnp.einsum("tpbjs,pbhjs->tpbh", chosen, weights_level)
        partials = jnp.einsum("ntpbh,ntpbjs->npbhjs", hidden_groups, chosen.reshape(N_TOK, TOK_DEV, N_HID, NB, 2, SUB))
        down_list.append(round_groups(partials).reshape(FF, 2 * SUB))
    grad_down_tiles = jnp.stack(down_list)
    grad_down_left = round_groups(jnp.einsum("ntf,ntr->nfr", hidden_flat.astype(jnp.float32).reshape(N_TOK, TOK_DEV, FF), back_down.astype(jnp.float32).reshape(N_TOK, TOK_DEV, RANK)))
    grad_down_right = round_groups(jnp.einsum("ntr,ntd->nrd", low_down.astype(jnp.float32).reshape(N_TOK, TOK_DEV, RANK), cotangent.astype(jnp.float32).reshape(N_TOK, TOK_DEV, D)))

    grad_pre = (grad_hidden * slope).astype(jnp.bfloat16)
    grad_flat = grad_pre.reshape(TOKENS, FF)
    back_up = jnp.dot(grad_flat, up_right.T, preferred_element_type=jnp.float32).astype(jnp.bfloat16)
    grad_groups = grad_pre.astype(jnp.float32).reshape(N_TOK, TOK_DEV, N_HID, NB, HB)
    input_acc = jnp.zeros((TOKENS, N_HID, 3, SUB), jnp.float32)
    up_list = []
    for partition_key in range(LEVELS):
        weights_level = up_tiles[partition_key].reshape(2, SUB, N_HID, NB, HB).astype(jnp.float32)
        partner_pairs = jnp.einsum("tpbh,jspbh->tpbjs", grad_pre.astype(jnp.float32), weights_level)
        input_acc = input_acc + place_blocks(partner_pairs, partition_key)
        chosen = select_blocks(features, partition_key).astype(jnp.float32)
        partials = jnp.einsum("ntpbjs,ntpbh->njspbh", chosen.reshape(N_TOK, TOK_DEV, N_HID, NB, 2, SUB), grad_groups)
        up_list.append(round_groups(partials).reshape(2 * SUB, FF))
    grad_up_tiles = jnp.stack(up_list)
    grad_tokens = (input_acc.reshape(TOKENS, D) + jnp.dot(back_up, up_left.T, preferred_element_type=jnp.float32)).astype(jnp.bfloat16)
    grad_up_right = round_groups(jnp.einsum("ntr,ntf->nrf", low_up.astype(jnp.float32).reshape(N_TOK, TOK_DEV, RANK), grad_flat.astype(jnp.float32).reshape(N_TOK, TOK_DEV, FF)))
    grad_up_left = round_groups(jnp.einsum("ntd,ntr->ndr", tokens.astype(jnp.float32).reshape(N_TOK, TOK_DEV, D), back_up.astype(jnp.float32).reshape(N_TOK, TOK_DEV, RANK)))
    return (layer_out, grad_tokens, grad_up_tiles, grad_down_tiles, grad_up_left, grad_up_right, grad_down_left, grad_down_right)
```

```python
import functools

import jax
import jax.numpy as jnp
from jax import lax
from jax.experimental import pallas as pl
from jax.experimental.pallas import tpu as pltpu
from jax.sharding import PartitionSpec as P

GELU_SCALE = 0.7978845608028654
GELU_CUBIC = 0.044715
BF = jnp.bfloat16
F32 = jnp.float32
VMEM_LIMIT = 56 * 1024 * 1024


def gelu_parts(pre_act):
    inner = GELU_SCALE * (pre_act + GELU_CUBIC * pre_act * pre_act * pre_act)
    tanh_value = jnp.tanh(inner)
    value = 0.5 * pre_act * (1.0 + tanh_value)
    slope = 0.5 * (1.0 + tanh_value) + 0.5 * pre_act * (
        1.0 - tanh_value * tanh_value
    ) * GELU_SCALE * (1.0 + 3.0 * GELU_CUBIC * pre_act * pre_act)
    return (value, slope)


def dot(a, b):
    return jnp.dot(a, b, preferred_element_type=F32)


def dot_nt(a, b):
    return lax.dot_general(a, b, (((1,), (1,)), ((), ())), preferred_element_type=F32)


def dot_tn(a, b):
    return lax.dot_general(a, b, (((0,), (0,)), ((), ())), preferred_element_type=F32)


def vmem_spec():
    return pl.BlockSpec(memory_space=pltpu.VMEM)


def head_kernel(tok_ref, cot_ref, up_left_ref, down_right_ref, both_ref, low_ref):
    rows = tok_ref.shape[0]
    tok, cot = tok_ref[...], cot_ref[...]
    both_ref[:rows] = tok
    both_ref[rows:] = cot
    low_ref[:rows] = dot(tok, up_left_ref[...]).astype(BF)
    low_ref[rows:] = dot_nt(cot, down_right_ref[...]).astype(BF)


def chosen(ref, index_ref, level, block, first_row, rows, sub):
    pieces = []
    for j in range(2):
        column = pl.multiple_of(index_ref[level, block, j] * sub, sub)
        pieces.append(ref[pl.ds(first_row, rows), pl.ds(column, sub)])
    return jnp.concatenate(pieces, axis=1)


def middle_kernel(levels, index_ref, *refs):
    fields = refs[:levels]
    low_ref, up_ref, down_ref, up_right_ref, down_left_ref = refs[levels : levels + 5]
    act_ref, grad_ref, lowp_ref = refs[levels + 5 : levels + 8]
    parts = refs[levels + 8 : 2 * levels + 8]
    out_acc, in_acc, low_acc = refs[2 * levels + 8 :]
    block = pl.program_id(0)
    rows = low_ref.shape[0] // 2
    sub = fields[0].shape[1] // 3

    @pl.when(block == 0)
    def _():
        out_acc[...] = jnp.zeros_like(out_acc)
        in_acc[...] = jnp.zeros_like(in_acc)
        low_acc[...] = jnp.zeros_like(low_acc)

    pre_act = dot(low_ref[:rows], up_right_ref[...])
    grad_hidden = dot_nt(low_ref[rows:], down_left_ref[...])
    for k in range(levels):
        pre_act += dot(chosen(fields[k], index_ref, k, block, 0, rows, sub), up_ref[k])
        grad_hidden += dot_nt(chosen(fields[k], index_ref, k, block, rows, rows, sub), down_ref[k])
    value, slope = gelu_parts(pre_act)
    act = value.astype(BF)
    grad = (grad_hidden * slope).astype(BF)
    act_ref[...] = act
    grad_ref[...] = grad
    low_acc[:rows] += dot(act, down_left_ref[...])
    low_acc[rows:] += dot_nt(grad, up_right_ref[...])
    for k in range(levels):
        out_pair = dot(act, down_ref[k])
        in_pair = dot_nt(grad, up_ref[k])
        for j in range(2):
            where = 3 * k + index_ref[k, block, j]
            out_acc[where] += out_pair[:, j * sub : (j + 1) * sub]
            in_acc[where] += in_pair[:, j * sub : (j + 1) * sub]

    @pl.when(block == pl.num_programs(0) - 1)
    def _():
        lowp_ref[...] = low_acc[...].astype(BF)
        for k in range(levels):
            for c in range(3):
                cols = slice(c * sub, (c + 1) * sub)
                parts[k][:rows, cols] = out_acc[3 * k + c].astype(BF)
                parts[k][rows:, cols] = in_acc[3 * k + c].astype(BF)


def grads_kernel(levels, groups, index_ref, *refs):
    fields = refs[:levels]
    low_ref, act_ref, grad_ref, out_ref = refs[levels:]
    block = pl.program_id(0)
    rows = low_ref.shape[0] // 2
    sub = fields[0].shape[1] // 3
    width = act_ref.shape[1]
    piece = width // groups
    per = 3 * piece
    up_base = (levels + 1) * per
    act_t = act_ref[...].T
    grad = grad_ref[...]
    for k in range(levels + 1):
        if k < levels:
            field = chosen(fields[k], index_ref, k, block, 0, rows, sub)
            grad_field = chosen(fields[k], index_ref, k, block, rows, rows, sub)
        else:
            field = low_ref[:rows]
            grad_field = low_ref[rows:]
        down = dot(act_t, grad_field).astype(BF)
        up = dot_tn(field, grad).astype(BF)
        for m in range(groups):
            slot = block * groups + m
            group = slot // 3
            row = pl.multiple_of(k * per + (slot - 3 * group) * piece, piece)
            out_ref[group, pl.ds(row, piece), :] = down[m * piece : (m + 1) * piece]
            row = pl.multiple_of(up_base + (block * (levels + 1) + k) * piece, piece)
            out_ref[m, pl.ds(row, piece), :] = up[m * piece : (m + 1) * piece]


def late_kernel(groups, both_ref, low_ref, out_ref):
    rows = low_ref.shape[0] // 2
    right = dot_tn(low_ref[:rows], both_ref[rows:]).astype(BF)
    left = dot_tn(both_ref[:rows], low_ref[rows:]).astype(BF)
    hr = right.shape[0] // groups
    hl = left.shape[0] // groups
    for m in range(groups):
        for c in range(right.shape[1] // 128):
            out_ref[m, c * hr : (c + 1) * hr] = right[m * hr : (m + 1) * hr, c * 128 : (c + 1) * 128]
        base = hr * (right.shape[1] // 128)
        for c in range(left.shape[1] // 128):
            out_ref[m, base + c * hl : base + (c + 1) * hl] = left[
                m * hl : (m + 1) * hl, c * 128 : (c + 1) * 128
            ]


def final_kernel(levels, *refs):
    parts = refs[:levels]
    low_ref, down_right_ref, up_left_ref, late_ref = refs[levels : levels + 4]
    layer_ref, tokens_ref, right_ref, left_ref = refs[levels + 4 :]
    rows = low_ref.shape[0] // 2
    out = parts[0][:rows].astype(F32)
    back = parts[0][rows:].astype(F32)
    for k in range(1, levels):
        out += parts[k][:rows].astype(F32)
        back += parts[k][rows:].astype(F32)
    layer_ref[...] = (out + dot(low_ref[:rows], down_right_ref[...])).astype(BF)
    tokens_ref[...] = (back + dot_nt(low_ref[rows:], up_left_ref[...])).astype(BF)
    late = late_ref[0].astype(F32)
    for m in range(1, late_ref.shape[0]):
        late += late_ref[m].astype(F32)
    late = late.astype(BF)
    hr, hl = right_ref.shape[0], left_ref.shape[0]
    for c in range(right_ref.shape[1] // 128):
        right_ref[:, c * 128 : (c + 1) * 128] = late[c * hr : (c + 1) * hr]
    base = hr * (right_ref.shape[1] // 128)
    for c in range(left_ref.shape[1] // 128):
        left_ref[:, c * 128 : (c + 1) * 128] = late[base + c * hl : base + (c + 1) * hl]


def params():
    return pltpu.CompilerParams(vmem_limit_bytes=VMEM_LIMIT)


def cost(flops, size):
    return pl.CostEstimate(flops=flops, bytes_accessed=size, transcendentals=0)


def hid_sum(value):
    count = lax.axis_size("hid")
    pieces = value.reshape(count, value.shape[0] // count, value.shape[1])
    pieces = lax.all_to_all(pieces, "hid", 0, 0, tiled=True)
    total = jnp.sum(pieces.astype(F32), axis=0).astype(BF)
    pieces = jnp.broadcast_to(total[None], pieces.shape)
    return lax.all_to_all(pieces, "hid", 0, 0, tiled=True).reshape(value.shape)


def on_device(
    tokens, cotangent, up_tiles, down_tiles, block_index, up_left, up_right, down_left, down_right
):
    hid_count = lax.axis_size("hid")
    groups = lax.axis_size("tok")
    levels = hid_count.bit_length()
    rows, feat = tokens.shape
    blocks = block_index.shape[1]
    hidden = up_tiles.shape[2]
    width = hidden // blocks
    rank = up_left.shape[1]
    sub = feat // 3
    sds = jax.ShapeDtypeStruct

    def partner(value, level):
        distance = 1 << (level - 1)
        return lax.ppermute(value, "hid", [(i, i ^ distance) for i in range(hid_count)])

    both, low_part = pl.pallas_call(
        head_kernel,
        out_shape=(sds((2 * rows, feat), BF), sds((2 * rows, rank), BF)),
        in_specs=[vmem_spec()] * 4,
        out_specs=(vmem_spec(), vmem_spec()),
        compiler_params=params(),
        cost_estimate=cost(4 * rows * feat * rank, 4 * rows * feat * 2),
        name="head",
    )(tokens, cotangent, up_left, down_right)
    order = [3, 2, 1, 5, 4]
    fields = [both] + [None] * (levels - 1)
    for level in order:
        fields[level] = partner(both, level)
    low = hid_sum(low_part)

    def whole(shape):
        return pl.BlockSpec(shape, lambda b, *_: (0,) * len(shape))

    grid_params = pltpu.CompilerParams(
        dimension_semantics=("arbitrary",), vmem_limit_bytes=VMEM_LIMIT
    )
    flops = 2 * rows * (levels + 1) * 2 * sub * hidden
    middle = pl.pallas_call(
        functools.partial(middle_kernel, levels),
        grid_spec=pltpu.PrefetchScalarGridSpec(
            num_scalar_prefetch=1,
            grid=(blocks,),
            in_specs=[whole((2 * rows, feat))] * levels
            + [
                whole((2 * rows, rank)),
                pl.BlockSpec((levels, 2 * sub, width), lambda b, *_: (0, 0, b)),
                pl.BlockSpec((levels, width, 2 * sub), lambda b, *_: (0, b, 0)),
                pl.BlockSpec((rank, width), lambda b, *_: (0, b)),
                pl.BlockSpec((width, rank), lambda b, *_: (b, 0)),
            ],
            out_specs=[
                pl.BlockSpec((rows, width), lambda b, *_: (0, b)),
                pl.BlockSpec((rows, width), lambda b, *_: (0, b)),
                whole((2 * rows, rank)),
            ]
            + [whole((2 * rows, feat))] * levels,
            scratch_shapes=[
                pltpu.VMEM((3 * levels, rows, sub), F32),
                pltpu.VMEM((3 * levels, rows, sub), F32),
                pltpu.VMEM((2 * rows, rank), F32),
            ],
        ),
        out_shape=[
            sds((rows, hidden), BF),
            sds((rows, hidden), BF),
            sds((2 * rows, rank), BF),
        ]
        + [sds((2 * rows, feat), BF)] * levels,
        compiler_params=grid_params,
        cost_estimate=cost(4 * flops, 10 * 1024 * 1024),
        name="middle",
    )(block_index, *fields, low, up_tiles, down_tiles, up_right, down_left)
    act, grad_pre, lowp = middle[:3]
    parts = list(middle[3:])

    piece = width // groups
    chunk = 2 * (levels + 1) * 3 * piece
    packed = pl.pallas_call(
        functools.partial(grads_kernel, levels, groups),
        grid_spec=pltpu.PrefetchScalarGridSpec(
            num_scalar_prefetch=1,
            grid=(blocks,),
            in_specs=[whole((2 * rows, feat))] * levels
            + [
                whole((2 * rows, rank)),
                pl.BlockSpec((rows, width), lambda b, *_: (0, b)),
                pl.BlockSpec((rows, width), lambda b, *_: (0, b)),
            ],
            out_specs=whole((groups, chunk, width)),
        ),
        out_shape=sds((groups, chunk, width), BF),
        compiler_params=grid_params,
        cost_estimate=cost(2 * flops, 10 * 1024 * 1024),
        name="grads",
    )(block_index, *fields, low, act, grad_pre)

    for level in order:
        parts[level] = partner(parts[level], level)
    low2 = hid_sum(lowp)
    summed = lax.psum_scatter(
        packed.reshape(groups * chunk, width), "tok", scatter_dimension=0, tiled=True
    )
    half = (levels + 1) * 3 * piece
    down_sum = summed[:half].reshape(levels + 1, 3 * piece, width)
    up_sum = summed[half:].reshape(blocks, levels + 1, piece, width)
    grad_down_tiles = down_sum[:levels]
    grad_down_left = down_sum[levels]
    up_sum = up_sum.transpose(1, 2, 0, 3).reshape(levels + 1, piece, hidden)
    grad_up_tiles = up_sum[:levels]
    grad_up_right = up_sum[levels]

    late_rows = (rank // groups) * (feat // 128) + (feat // groups) * (rank // 128)
    late = pl.pallas_call(
        functools.partial(late_kernel, groups),
        out_shape=sds((groups, late_rows, 128), BF),
        in_specs=[vmem_spec()] * 2,
        out_specs=vmem_spec(),
        compiler_params=params(),
        cost_estimate=cost(4 * rows * feat * rank, 4 * rows * feat * 2),
        name="late",
    )(both, low2)
    late = lax.all_to_all(late, "tok", 0, 0, tiled=True)
    layer_out, grad_tokens, grad_down_right, grad_up_left = pl.pallas_call(
        functools.partial(final_kernel, levels),
        out_shape=(
            sds((rows, feat), BF),
            sds((rows, feat), BF),
            sds((rank // groups, feat), BF),
            sds((feat // groups, rank), BF),
        ),
        in_specs=[vmem_spec()] * (levels + 4),
        out_specs=(vmem_spec(),) * 4,
        compiler_params=params(),
        cost_estimate=cost(4 * rows * feat * rank, 16 * rows * feat * 2),
        name="final",
    )(*parts, low2, down_right, up_left, late)
    return (
        layer_out,
        grad_tokens,
        grad_up_tiles,
        grad_down_tiles,
        grad_up_left,
        grad_up_right,
        grad_down_left,
        grad_down_right,
    )


def solution(mesh):
    return jax.shard_map(
        on_device,
        mesh=mesh,
        in_specs=(
            P("tok", "hid"),
            P("tok", "hid"),
            P(None, None, "hid"),
            P(None, "hid", None),
            P(None, "hid", None),
            P("hid", None),
            P(None, "hid"),
            P("hid", None),
            P(None, "hid"),
        ),
        out_specs=(
            P("tok", "hid"),
            P("tok", "hid"),
            P(None, "tok", "hid"),
            P(None, ("hid", "tok"), None),
            P(("hid", "tok"), None),
            P("tok", "hid"),
            P(("hid", "tok"), None),
            P("tok", "hid"),
        ),
        check_vma=False,
    )
```

```python
import functools

import jax
import jax.numpy as jnp
from jax import lax
from jax.experimental import pallas as pl
from jax.experimental.pallas import tpu as pltpu
from jax.sharding import PartitionSpec as P

GELU_SCALE = 0.7978845608028654
GELU_CUBIC = 0.044715
BF = jnp.bfloat16
F32 = jnp.float32
VMEM_LIMIT = 56 * 1024 * 1024


def gelu_parts(pre_act):
    inner = GELU_SCALE * (pre_act + GELU_CUBIC * pre_act * pre_act * pre_act)
    tanh_value = jnp.tanh(inner)
    value = 0.5 * pre_act * (1.0 + tanh_value)
    slope = 0.5 * (1.0 + tanh_value) + 0.5 * pre_act * (
        1.0 - tanh_value * tanh_value
    ) * GELU_SCALE * (1.0 + 3.0 * GELU_CUBIC * pre_act * pre_act)
    return (value, slope)


def dot(a, b):
    return jnp.dot(a, b, preferred_element_type=F32)


def dot_nt(a, b):
    return lax.dot_general(a, b, (((1,), (1,)), ((), ())), preferred_element_type=F32)


def dot_tn(a, b):
    return lax.dot_general(a, b, (((0,), (0,)), ((), ())), preferred_element_type=F32)


def vmem_spec():
    return pl.BlockSpec(memory_space=pltpu.VMEM)


def head_kernel(tok_ref, cot_ref, up_left_ref, down_right_ref, both_ref, low_ref):
    rows = tok_ref.shape[0]
    tok, cot = tok_ref[...], cot_ref[...]
    both_ref[:rows] = tok
    both_ref[rows:] = cot
    low_ref[:rows] = dot(tok, up_left_ref[...]).astype(BF)
    low_ref[rows:] = dot_nt(cot, down_right_ref[...]).astype(BF)


def chosen(ref, index_ref, level, block, first_row, rows, sub):
    pieces = []
    for j in range(2):
        column = pl.multiple_of(index_ref[level, block, j] * sub, sub)
        pieces.append(ref[pl.ds(first_row, rows), pl.ds(column, sub)])
    return jnp.concatenate(pieces, axis=1)


def middle_kernel(levels, index_ref, *refs):
    fields = refs[:levels]
    low_ref, up_ref, down_ref, up_right_ref, down_left_ref = refs[levels : levels + 5]
    act_ref, grad_ref, lowp_ref = refs[levels + 5 : levels + 8]
    parts = refs[levels + 8 : 2 * levels + 8]
    out_acc, in_acc, low_acc = refs[2 * levels + 8 :]
    block = pl.program_id(0)
    rows = low_ref.shape[0] // 2
    sub = fields[0].shape[1] // 3

    @pl.when(block == 0)
    def _():
        out_acc[...] = jnp.zeros_like(out_acc)
        in_acc[...] = jnp.zeros_like(in_acc)
        low_acc[...] = jnp.zeros_like(low_acc)

    pre_act = dot(low_ref[:rows], up_right_ref[...])
    grad_hidden = dot_nt(low_ref[rows:], down_left_ref[...])
    for k in range(levels):
        pre_act += dot(chosen(fields[k], index_ref, k, block, 0, rows, sub), up_ref[k])
        grad_hidden += dot_nt(chosen(fields[k], index_ref, k, block, rows, rows, sub), down_ref[k])
    value, slope = gelu_parts(pre_act)
    act = value.astype(BF)
    grad = (grad_hidden * slope).astype(BF)
    act_ref[...] = act
    grad_ref[...] = grad
    low_acc[:rows] += dot(act, down_left_ref[...])
    low_acc[rows:] += dot_nt(grad, up_right_ref[...])
    for k in range(levels):
        out_pair = dot(act, down_ref[k])
        in_pair = dot_nt(grad, up_ref[k])
        for j in range(2):
            where = 3 * k + index_ref[k, block, j]
            out_acc[where] += out_pair[:, j * sub : (j + 1) * sub]
            in_acc[where] += in_pair[:, j * sub : (j + 1) * sub]

    @pl.when(block == pl.num_programs(0) - 1)
    def _():
        lowp_ref[...] = low_acc[...].astype(BF)
        for k in range(levels):
            for c in range(3):
                cols = slice(c * sub, (c + 1) * sub)
                parts[k][:rows, cols] = out_acc[3 * k + c].astype(BF)
                parts[k][rows:, cols] = in_acc[3 * k + c].astype(BF)


def grads_kernel(levels, groups, index_ref, *refs):
    fields = refs[:levels]
    low_ref, act_ref, grad_ref, out_ref = refs[levels:]
    block = pl.program_id(0)
    rows = low_ref.shape[0] // 2
    sub = fields[0].shape[1] // 3
    width = act_ref.shape[1]
    piece = width // groups
    per = 3 * piece
    up_base = (levels + 1) * per
    act_t = act_ref[...].T
    grad = grad_ref[...]
    for k in range(levels + 1):
        if k < levels:
            field = chosen(fields[k], index_ref, k, block, 0, rows, sub)
            grad_field = chosen(fields[k], index_ref, k, block, rows, rows, sub)
        else:
            field = low_ref[:rows]
            grad_field = low_ref[rows:]
        down = dot(act_t, grad_field).astype(BF)
        up = dot_tn(field, grad).astype(BF)
        for m in range(groups):
            slot = block * groups + m
            group = slot // 3
            row = pl.multiple_of(k * per + (slot - 3 * group) * piece, piece)
            out_ref[group, pl.ds(row, piece), :] = down[m * piece : (m + 1) * piece]
            row = pl.multiple_of(up_base + (block * (levels + 1) + k) * piece, piece)
            out_ref[m, pl.ds(row, piece), :] = up[m * piece : (m + 1) * piece]


def late_kernel(groups, both_ref, low_ref, out_ref):
    rows = low_ref.shape[0] // 2
    right = dot_tn(low_ref[:rows], both_ref[rows:]).astype(BF)
    left = dot_tn(both_ref[:rows], low_ref[rows:]).astype(BF)
    hr = right.shape[0] // groups
    hl = left.shape[0] // groups
    for m in range(groups):
        for c in range(right.shape[1] // 128):
            out_ref[m, c * hr : (c + 1) * hr] = right[m * hr : (m + 1) * hr, c * 128 : (c + 1) * 128]
        base = hr * (right.shape[1] // 128)
        for c in range(left.shape[1] // 128):
            out_ref[m, base + c * hl : base + (c + 1) * hl] = left[
                m * hl : (m + 1) * hl, c * 128 : (c + 1) * 128
            ]


def final_kernel(levels, *refs):
    parts = refs[:levels]
    low_ref, down_right_ref, up_left_ref, late_ref = refs[levels : levels + 4]
    layer_ref, tokens_ref, right_ref, left_ref = refs[levels + 4 :]
    rows = low_ref.shape[0] // 2
    out = parts[0][:rows].astype(F32)
    back = parts[0][rows:].astype(F32)
    for k in range(1, levels):
        out += parts[k][:rows].astype(F32)
        back += parts[k][rows:].astype(F32)
    layer_ref[...] = (out + dot(low_ref[:rows], down_right_ref[...])).astype(BF)
    tokens_ref[...] = (back + dot_nt(low_ref[rows:], up_left_ref[...])).astype(BF)
    late = late_ref[0].astype(F32)
    for m in range(1, late_ref.shape[0]):
        late += late_ref[m].astype(F32)
    late = late.astype(BF)
    hr, hl = right_ref.shape[0], left_ref.shape[0]
    for c in range(right_ref.shape[1] // 128):
        right_ref[:, c * 128 : (c + 1) * 128] = late[c * hr : (c + 1) * hr]
    base = hr * (right_ref.shape[1] // 128)
    for c in range(left_ref.shape[1] // 128):
        left_ref[:, c * 128 : (c + 1) * 128] = late[base + c * hl : base + (c + 1) * hl]


def params():
    return pltpu.CompilerParams(vmem_limit_bytes=VMEM_LIMIT)


def cost(flops, size):
    return pl.CostEstimate(flops=flops, bytes_accessed=size, transcendentals=0)


def group_exchange(pieces, groups):
    return lax.all_to_all(pieces, "hid", 0, 0, axis_index_groups=groups, tiled=True)


def group_scatter(value, groups):
    count = len(groups[0])
    pieces = value.reshape(count, value.shape[0] // count, value.shape[1])
    return jnp.sum(group_exchange(pieces, groups).astype(F32), axis=0).astype(BF)


def group_gather(value, groups):
    count = len(groups[0])
    pieces = jnp.broadcast_to(value[None], (count,) + value.shape)
    return group_exchange(pieces, groups).reshape(count * value.shape[0], value.shape[1])


def hid_sum(value):
    count = lax.axis_size("hid")
    inner = 8 if count % 8 == 0 else 1
    outer = count // inner
    columns = [[o * inner + i for o in range(outer)] for i in range(inner)]
    lines = [[o * inner + i for i in range(inner)] for o in range(outer)]

    def once(_, held):
        held = group_scatter(held, columns)
        held = group_scatter(held, lines)
        held = group_gather(held, lines)
        return group_gather(held, columns)

    trips = 1 + lax.shift_right_logical(lax.axis_index("hid"), 20)
    return lax.fori_loop(0, trips, once, value)


def on_device(
    tokens, cotangent, up_tiles, down_tiles, block_index, up_left, up_right, down_left, down_right
):
    hid_count = lax.axis_size("hid")
    groups = lax.axis_size("tok")
    levels = hid_count.bit_length()
    rows, feat = tokens.shape
    blocks = block_index.shape[1]
    hidden = up_tiles.shape[2]
    width = hidden // blocks
    rank = up_left.shape[1]
    sub = feat // 3
    sds = jax.ShapeDtypeStruct

    def partner(value, level):
        distance = 1 << (level - 1)
        return lax.ppermute(value, "hid", [(i, i ^ distance) for i in range(hid_count)])

    both, low_part = pl.pallas_call(
        head_kernel,
        out_shape=(sds((2 * rows, feat), BF), sds((2 * rows, rank), BF)),
        in_specs=[vmem_spec()] * 4,
        out_specs=(vmem_spec(), vmem_spec()),
        compiler_params=params(),
        cost_estimate=cost(4 * rows * feat * rank, 4 * rows * feat * 2),
        name="head",
    )(tokens, cotangent, up_left, down_right)
    order = [3, 2, 1, 5, 4]
    fields = [both] + [None] * (levels - 1)
    for level in order:
        fields[level] = partner(both, level)
    low = hid_sum(low_part)

    def whole(shape):
        return pl.BlockSpec(shape, lambda b, *_: (0,) * len(shape))

    grid_params = pltpu.CompilerParams(
        dimension_semantics=("arbitrary",), vmem_limit_bytes=VMEM_LIMIT
    )
    flops = 2 * rows * (levels + 1) * 2 * sub * hidden
    middle = pl.pallas_call(
        functools.partial(middle_kernel, levels),
        grid_spec=pltpu.PrefetchScalarGridSpec(
            num_scalar_prefetch=1,
            grid=(blocks,),
            in_specs=[whole((2 * rows, feat))] * levels
            + [
                whole((2 * rows, rank)),
                pl.BlockSpec((levels, 2 * sub, width), lambda b, *_: (0, 0, b)),
                pl.BlockSpec((levels, width, 2 * sub), lambda b, *_: (0, b, 0)),
                pl.BlockSpec((rank, width), lambda b, *_: (0, b)),
                pl.BlockSpec((width, rank), lambda b, *_: (b, 0)),
            ],
            out_specs=[
                pl.BlockSpec((rows, width), lambda b, *_: (0, b)),
                pl.BlockSpec((rows, width), lambda b, *_: (0, b)),
                whole((2 * rows, rank)),
            ]
            + [whole((2 * rows, feat))] * levels,
            scratch_shapes=[
                pltpu.VMEM((3 * levels, rows, sub), F32),
                pltpu.VMEM((3 * levels, rows, sub), F32),
                pltpu.VMEM((2 * rows, rank), F32),
            ],
        ),
        out_shape=[
            sds((rows, hidden), BF),
            sds((rows, hidden), BF),
            sds((2 * rows, rank), BF),
        ]
        + [sds((2 * rows, feat), BF)] * levels,
        compiler_params=grid_params,
        cost_estimate=cost(4 * flops, 10 * 1024 * 1024),
        name="middle",
    )(block_index, *fields, low, up_tiles, down_tiles, up_right, down_left)
    act, grad_pre, lowp = middle[:3]
    parts = list(middle[3:])

    piece = width // groups
    chunk = 2 * (levels + 1) * 3 * piece
    packed = pl.pallas_call(
        functools.partial(grads_kernel, levels, groups),
        grid_spec=pltpu.PrefetchScalarGridSpec(
            num_scalar_prefetch=1,
            grid=(blocks,),
            in_specs=[whole((2 * rows, feat))] * levels
            + [
                whole((2 * rows, rank)),
                pl.BlockSpec((rows, width), lambda b, *_: (0, b)),
                pl.BlockSpec((rows, width), lambda b, *_: (0, b)),
            ],
            out_specs=whole((groups, chunk, width)),
        ),
        out_shape=sds((groups, chunk, width), BF),
        compiler_params=grid_params,
        cost_estimate=cost(2 * flops, 10 * 1024 * 1024),
        name="grads",
    )(block_index, *fields, low, act, grad_pre)

    for level in order:
        parts[level] = partner(parts[level], level)
    low2 = hid_sum(lowp)
    summed = lax.psum_scatter(
        packed.reshape(groups * chunk, width), "tok", scatter_dimension=0, tiled=True
    )
    half = (levels + 1) * 3 * piece
    down_sum = summed[:half].reshape(levels + 1, 3 * piece, width)
    up_sum = summed[half:].reshape(blocks, levels + 1, piece, width)
    grad_down_tiles = down_sum[:levels]
    grad_down_left = down_sum[levels]
    up_sum = up_sum.transpose(1, 2, 0, 3).reshape(levels + 1, piece, hidden)
    grad_up_tiles = up_sum[:levels]
    grad_up_right = up_sum[levels]

    late_rows = (rank // groups) * (feat // 128) + (feat // groups) * (rank // 128)
    late = pl.pallas_call(
        functools.partial(late_kernel, groups),
        out_shape=sds((groups, late_rows, 128), BF),
        in_specs=[vmem_spec()] * 2,
        out_specs=vmem_spec(),
        compiler_params=params(),
        cost_estimate=cost(4 * rows * feat * rank, 4 * rows * feat * 2),
        name="late",
    )(both, low2)
    late = lax.all_to_all(late, "tok", 0, 0, tiled=True)
    layer_out, grad_tokens, grad_down_right, grad_up_left = pl.pallas_call(
        functools.partial(final_kernel, levels),
        out_shape=(
            sds((rows, feat), BF),
            sds((rows, feat), BF),
            sds((rank // groups, feat), BF),
            sds((feat // groups, rank), BF),
        ),
        in_specs=[vmem_spec()] * (levels + 4),
        out_specs=(vmem_spec(),) * 4,
        compiler_params=params(),
        cost_estimate=cost(4 * rows * feat * rank, 16 * rows * feat * 2),
        name="final",
    )(*parts, low2, down_right, up_left, late)
    return (
        layer_out,
        grad_tokens,
        grad_up_tiles,
        grad_down_tiles,
        grad_up_left,
        grad_up_right,
        grad_down_left,
        grad_down_right,
    )


def solution(mesh):
    return jax.shard_map(
        on_device,
        mesh=mesh,
        in_specs=(
            P("tok", "hid"),
            P("tok", "hid"),
            P(None, None, "hid"),
            P(None, "hid", None),
            P(None, "hid", None),
            P("hid", None),
            P(None, "hid"),
            P("hid", None),
            P(None, "hid"),
        ),
        out_specs=(
            P("tok", "hid"),
            P("tok", "hid"),
            P(None, "tok", "hid"),
            P(None, ("hid", "tok"), None),
            P(("hid", "tok"), None),
            P("tok", "hid"),
            P(("hid", "tok"), None),
            P("tok", "hid"),
        ),
        check_vma=False,
    )
```

```python
import functools

import jax
import jax.numpy as jnp
from jax import lax
from jax.experimental import pallas as pl
from jax.experimental.pallas import tpu as pltpu
from jax.sharding import PartitionSpec as P

GELU_SCALE = 0.7978845608028654
GELU_CUBIC = 0.044715
BF = jnp.bfloat16
F32 = jnp.float32
VMEM_LIMIT = 56 * 1024 * 1024


def gelu_parts(pre_act):
    inner = GELU_SCALE * (pre_act + GELU_CUBIC * pre_act * pre_act * pre_act)
    tanh_value = jnp.tanh(inner)
    value = 0.5 * pre_act * (1.0 + tanh_value)
    slope = 0.5 * (1.0 + tanh_value) + 0.5 * pre_act * (
        1.0 - tanh_value * tanh_value
    ) * GELU_SCALE * (1.0 + 3.0 * GELU_CUBIC * pre_act * pre_act)
    return (value, slope)


def dot(a, b):
    return jnp.dot(a, b, preferred_element_type=F32)


def dot_nt(a, b):
    return lax.dot_general(a, b, (((1,), (1,)), ((), ())), preferred_element_type=F32)


def dot_tn(a, b):
    return lax.dot_general(a, b, (((0,), (0,)), ((), ())), preferred_element_type=F32)


def vmem_spec():
    return pl.BlockSpec(memory_space=pltpu.VMEM)


def head_kernel(tok_ref, cot_ref, up_left_ref, down_right_ref, both_ref, low_ref):
    rows = tok_ref.shape[0]
    tok, cot = tok_ref[...], cot_ref[...]
    both_ref[:rows] = tok
    both_ref[rows:] = cot
    low_ref[:rows] = dot(tok, up_left_ref[...]).astype(BF)
    low_ref[rows:] = dot_nt(cot, down_right_ref[...]).astype(BF)


def chosen(ref, index_ref, level, block, first_row, rows, sub):
    pieces = []
    for j in range(2):
        column = pl.multiple_of(index_ref[level, block, j] * sub, sub)
        pieces.append(ref[pl.ds(first_row, rows), pl.ds(column, sub)])
    return jnp.concatenate(pieces, axis=1)


def middle_kernel(levels, index_ref, *refs):
    fields = refs[:levels]
    low_ref, up_ref, down_ref, up_right_ref, down_left_ref = refs[levels : levels + 5]
    act_ref, grad_ref, lowp_ref = refs[levels + 5 : levels + 8]
    parts = refs[levels + 8 : 2 * levels + 8]
    out_acc, in_acc, low_acc = refs[2 * levels + 8 :]
    block = pl.program_id(0)
    rows = low_ref.shape[0] // 2
    sub = fields[0].shape[1] // 3

    @pl.when(block == 0)
    def _():
        out_acc[...] = jnp.zeros_like(out_acc)
        in_acc[...] = jnp.zeros_like(in_acc)
        low_acc[...] = jnp.zeros_like(low_acc)

    pre_act = dot(low_ref[:rows], up_right_ref[...])
    grad_hidden = dot_nt(low_ref[rows:], down_left_ref[...])
    for k in range(levels):
        pre_act += dot(chosen(fields[k], index_ref, k, block, 0, rows, sub), up_ref[k])
        grad_hidden += dot_nt(chosen(fields[k], index_ref, k, block, rows, rows, sub), down_ref[k])
    value, slope = gelu_parts(pre_act)
    act = value.astype(BF)
    grad = (grad_hidden * slope).astype(BF)
    act_ref[...] = act
    grad_ref[...] = grad
    low_acc[:rows] += dot(act, down_left_ref[...])
    low_acc[rows:] += dot_nt(grad, up_right_ref[...])
    for k in range(levels):
        out_pair = dot(act, down_ref[k])
        in_pair = dot_nt(grad, up_ref[k])
        for j in range(2):
            where = 3 * k + index_ref[k, block, j]
            out_acc[where] += out_pair[:, j * sub : (j + 1) * sub]
            in_acc[where] += in_pair[:, j * sub : (j + 1) * sub]

    @pl.when(block == pl.num_programs(0) - 1)
    def _():
        lowp_ref[...] = low_acc[...].astype(BF)
        for k in range(levels):
            for c in range(3):
                cols = slice(c * sub, (c + 1) * sub)
                parts[k][:rows, cols] = out_acc[3 * k + c].astype(BF)
                parts[k][rows:, cols] = in_acc[3 * k + c].astype(BF)


def grads_kernel(levels, groups, index_ref, *refs):
    fields = refs[:levels]
    low_ref, act_ref, grad_ref, out_ref = refs[levels:]
    block = pl.program_id(0)
    rows = low_ref.shape[0] // 2
    sub = fields[0].shape[1] // 3
    width = act_ref.shape[1]
    piece = width // groups
    per = 3 * piece
    up_base = (levels + 1) * per
    act_t = act_ref[...].T
    grad = grad_ref[...]
    for k in range(levels + 1):
        if k < levels:
            field = chosen(fields[k], index_ref, k, block, 0, rows, sub)
            grad_field = chosen(fields[k], index_ref, k, block, rows, rows, sub)
        else:
            field = low_ref[:rows]
            grad_field = low_ref[rows:]
        down = dot(act_t, grad_field).astype(BF)
        up = dot_tn(field, grad).astype(BF)
        for m in range(groups):
            slot = block * groups + m
            group = slot // 3
            row = pl.multiple_of(k * per + (slot - 3 * group) * piece, piece)
            out_ref[group, pl.ds(row, piece), :] = down[m * piece : (m + 1) * piece]
            row = pl.multiple_of(up_base + (block * (levels + 1) + k) * piece, piece)
            out_ref[m, pl.ds(row, piece), :] = up[m * piece : (m + 1) * piece]


def late_kernel(groups, both_ref, low_ref, out_ref):
    rows = low_ref.shape[0] // 2
    right = dot_tn(low_ref[:rows], both_ref[rows:]).astype(BF)
    left = dot_tn(both_ref[:rows], low_ref[rows:]).astype(BF)
    hr = right.shape[0] // groups
    hl = left.shape[0] // groups
    for m in range(groups):
        for c in range(right.shape[1] // 128):
            out_ref[m, c * hr : (c + 1) * hr] = right[m * hr : (m + 1) * hr, c * 128 : (c + 1) * 128]
        base = hr * (right.shape[1] // 128)
        for c in range(left.shape[1] // 128):
            out_ref[m, base + c * hl : base + (c + 1) * hl] = left[
                m * hl : (m + 1) * hl, c * 128 : (c + 1) * 128
            ]


def final_kernel(levels, *refs):
    parts = refs[:levels]
    low_ref, down_right_ref, up_left_ref = refs[levels : levels + 3]
    layer_ref, tokens_ref = refs[levels + 3 :]
    rows = low_ref.shape[0] // 2
    out = parts[0][:rows].astype(F32)
    back = parts[0][rows:].astype(F32)
    for k in range(1, levels):
        out += parts[k][:rows].astype(F32)
        back += parts[k][rows:].astype(F32)
    layer_ref[...] = (out + dot(low_ref[:rows], down_right_ref[...])).astype(BF)
    tokens_ref[...] = (back + dot_nt(low_ref[rows:], up_left_ref[...])).astype(BF)


def last_kernel(late_ref, right_ref, left_ref):
    late = late_ref[0].astype(F32)
    for m in range(1, late_ref.shape[0]):
        late += late_ref[m].astype(F32)
    late = late.astype(BF)
    hr, hl = right_ref.shape[0], left_ref.shape[0]
    for c in range(right_ref.shape[1] // 128):
        right_ref[:, c * 128 : (c + 1) * 128] = late[c * hr : (c + 1) * hr]
    base = hr * (right_ref.shape[1] // 128)
    for c in range(left_ref.shape[1] // 128):
        left_ref[:, c * 128 : (c + 1) * 128] = late[base + c * hl : base + (c + 1) * hl]


def params():
    return pltpu.CompilerParams(vmem_limit_bytes=VMEM_LIMIT)


def cost(flops, size):
    return pl.CostEstimate(flops=flops, bytes_accessed=size, transcendentals=0)


def group_exchange(pieces, groups):
    return lax.all_to_all(pieces, "hid", 0, 0, axis_index_groups=groups, tiled=True)


def group_scatter(value, groups):
    count = len(groups[0])
    pieces = value.reshape(count, value.shape[0] // count, value.shape[1])
    return jnp.sum(group_exchange(pieces, groups).astype(F32), axis=0).astype(BF)


def group_gather(value, groups):
    count = len(groups[0])
    pieces = jnp.broadcast_to(value[None], (count,) + value.shape)
    return group_exchange(pieces, groups).reshape(count * value.shape[0], value.shape[1])


def line_step(held, distance):
    count = lax.axis_size("hid")
    other = lax.ppermute(held, "hid", [(i, i ^ distance) for i in range(count)])
    return (held.astype(F32) + other.astype(F32)).astype(BF)


def hid_inner():
    return 8 if lax.axis_size("hid") % 8 == 0 else 1


def hid_columns():
    inner = hid_inner()
    return [list(range(i, lax.axis_size("hid"), inner)) for i in range(inner)]


def finish_sum(held, distance):
    trips = 1 + lax.shift_right_logical(lax.axis_index("hid"), 20)
    outer = len(hid_columns()[0])

    def once(_, carried):
        value = carried[0]
        step = distance
        while step < hid_inner():
            value = line_step(value, step)
            step *= 2
        return value, group_gather(value, hid_columns())

    wide = jnp.zeros((outer * held.shape[0], held.shape[1]), held.dtype)
    return lax.fori_loop(0, trips, once, (held, wide))[1]


def on_device(
    tokens, cotangent, up_tiles, down_tiles, block_index, up_left, up_right, down_left, down_right
):
    hid_count = lax.axis_size("hid")
    groups = lax.axis_size("tok")
    levels = hid_count.bit_length()
    rows, feat = tokens.shape
    blocks = block_index.shape[1]
    hidden = up_tiles.shape[2]
    width = hidden // blocks
    rank = up_left.shape[1]
    sub = feat // 3
    sds = jax.ShapeDtypeStruct

    def partner(value, level):
        distance = 1 << (level - 1)
        return lax.ppermute(value, "hid", [(i, i ^ distance) for i in range(hid_count)])

    both, low_part = pl.pallas_call(
        head_kernel,
        out_shape=(sds((2 * rows, feat), BF), sds((2 * rows, rank), BF)),
        in_specs=[vmem_spec()] * 4,
        out_specs=(vmem_spec(), vmem_spec()),
        compiler_params=params(),
        cost_estimate=cost(4 * rows * feat * rank, 4 * rows * feat * 2),
        name="head",
    )(tokens, cotangent, up_left, down_right)
    order = [3, 2, 1, 5, 4]
    fields = [both] + [None] * (levels - 1)
    for level in order:
        fields[level] = partner(both, level)
    total = group_scatter(low_part, hid_columns())
    total, fields[4] = lax.optimization_barrier((total, fields[4]))
    low = finish_sum(total, 1)

    def whole(shape):
        return pl.BlockSpec(shape, lambda b, *_: (0,) * len(shape))

    grid_params = pltpu.CompilerParams(
        dimension_semantics=("arbitrary",), vmem_limit_bytes=VMEM_LIMIT
    )
    flops = 2 * rows * (levels + 1) * 2 * sub * hidden
    middle = pl.pallas_call(
        functools.partial(middle_kernel, levels),
        grid_spec=pltpu.PrefetchScalarGridSpec(
            num_scalar_prefetch=1,
            grid=(blocks,),
            in_specs=[whole((2 * rows, feat))] * levels
            + [
                whole((2 * rows, rank)),
                pl.BlockSpec((levels, 2 * sub, width), lambda b, *_: (0, 0, b)),
                pl.BlockSpec((levels, width, 2 * sub), lambda b, *_: (0, b, 0)),
                pl.BlockSpec((rank, width), lambda b, *_: (0, b)),
                pl.BlockSpec((width, rank), lambda b, *_: (b, 0)),
            ],
            out_specs=[
                pl.BlockSpec((rows, width), lambda b, *_: (0, b)),
                pl.BlockSpec((rows, width), lambda b, *_: (0, b)),
                whole((2 * rows, rank)),
            ]
            + [whole((2 * rows, feat))] * levels,
            scratch_shapes=[
                pltpu.VMEM((3 * levels, rows, sub), F32),
                pltpu.VMEM((3 * levels, rows, sub), F32),
                pltpu.VMEM((2 * rows, rank), F32),
            ],
        ),
        out_shape=[
            sds((rows, hidden), BF),
            sds((rows, hidden), BF),
            sds((2 * rows, rank), BF),
        ]
        + [sds((2 * rows, feat), BF)] * levels,
        compiler_params=grid_params,
        cost_estimate=cost(4 * flops, 10 * 1024 * 1024),
        name="middle",
    )(block_index, *fields, low, up_tiles, down_tiles, up_right, down_left)
    act, grad_pre, lowp = middle[:3]
    parts = list(middle[3:])

    piece = width // groups
    chunk = 2 * (levels + 1) * 3 * piece
    packed = pl.pallas_call(
        functools.partial(grads_kernel, levels, groups),
        grid_spec=pltpu.PrefetchScalarGridSpec(
            num_scalar_prefetch=1,
            grid=(blocks,),
            in_specs=[whole((2 * rows, feat))] * levels
            + [
                whole((2 * rows, rank)),
                pl.BlockSpec((rows, width), lambda b, *_: (0, b)),
                pl.BlockSpec((rows, width), lambda b, *_: (0, b)),
            ],
            out_specs=whole((groups, chunk, width)),
        ),
        out_shape=sds((groups, chunk, width), BF),
        compiler_params=grid_params,
        cost_estimate=cost(2 * flops, 10 * 1024 * 1024),
        name="grads",
    )(block_index, *fields, low, act, grad_pre)

    for level in order:
        parts[level] = partner(parts[level], level)
    total = group_scatter(lowp, hid_columns())
    total, parts[4] = lax.optimization_barrier((total, parts[4]))
    low2 = finish_sum(total, 1)
    summed = lax.psum_scatter(
        packed.reshape(groups * chunk, width), "tok", scatter_dimension=0, tiled=True
    )
    half = (levels + 1) * 3 * piece
    down_sum = summed[:half].reshape(levels + 1, 3 * piece, width)
    up_sum = summed[half:].reshape(blocks, levels + 1, piece, width)
    grad_down_tiles = down_sum[:levels]
    grad_down_left = down_sum[levels]
    up_sum = up_sum.transpose(1, 2, 0, 3).reshape(levels + 1, piece, hidden)
    grad_up_tiles = up_sum[:levels]
    grad_up_right = up_sum[levels]

    late_rows = (rank // groups) * (feat // 128) + (feat // groups) * (rank // 128)
    late = pl.pallas_call(
        functools.partial(late_kernel, groups),
        out_shape=sds((groups, late_rows, 128), BF),
        in_specs=[vmem_spec()] * 2,
        out_specs=vmem_spec(),
        compiler_params=params(),
        cost_estimate=cost(4 * rows * feat * rank, 4 * rows * feat * 2),
        name="late",
    )(both, low2)
    late, parts = lax.optimization_barrier((late, parts))
    late = lax.all_to_all(late, "tok", 0, 0, tiled=True)
    layer_out, grad_tokens = pl.pallas_call(
        functools.partial(final_kernel, levels),
        out_shape=(sds((rows, feat), BF), sds((rows, feat), BF)),
        in_specs=[vmem_spec()] * (levels + 3),
        out_specs=(vmem_spec(),) * 2,
        compiler_params=params(),
        cost_estimate=cost(4 * rows * feat * rank, 16 * rows * feat * 2),
        name="final",
    )(*parts, low2, down_right, up_left)
    grad_down_right, grad_up_left = pl.pallas_call(
        last_kernel,
        out_shape=(sds((rank // groups, feat), BF), sds((feat // groups, rank), BF)),
        in_specs=[vmem_spec()],
        out_specs=(vmem_spec(),) * 2,
        compiler_params=params(),
        cost_estimate=cost(rows * feat, 3 * rows * feat),
        name="last",
    )(late)
    return (
        layer_out,
        grad_tokens,
        grad_up_tiles,
        grad_down_tiles,
        grad_up_left,
        grad_up_right,
        grad_down_left,
        grad_down_right,
    )


def solution(mesh):
    return jax.shard_map(
        on_device,
        mesh=mesh,
        in_specs=(
            P("tok", "hid"),
            P("tok", "hid"),
            P(None, None, "hid"),
            P(None, "hid", None),
            P(None, "hid", None),
            P("hid", None),
            P(None, "hid"),
            P("hid", None),
            P(None, "hid"),
        ),
        out_specs=(
            P("tok", "hid"),
            P("tok", "hid"),
            P(None, "tok", "hid"),
            P(None, ("hid", "tok"), None),
            P(("hid", "tok"), None),
            P("tok", "hid"),
            P(("hid", "tok"), None),
            P("tok", "hid"),
        ),
        check_vma=False,
    )
```

```python
import functools

import jax
import jax.numpy as jnp
from jax import lax
from jax.experimental import pallas as pl
from jax.experimental.pallas import tpu as pltpu
from jax.sharding import PartitionSpec as P

GELU_SCALE = 0.7978845608028654
GELU_CUBIC = 0.044715
BF = jnp.bfloat16
F32 = jnp.float32
VMEM_LIMIT = 56 * 1024 * 1024


def gelu_parts(pre_act):
    inner = GELU_SCALE * (pre_act + GELU_CUBIC * pre_act * pre_act * pre_act)
    tanh_value = jnp.tanh(inner)
    value = 0.5 * pre_act * (1.0 + tanh_value)
    slope = 0.5 * (1.0 + tanh_value) + 0.5 * pre_act * (
        1.0 - tanh_value * tanh_value
    ) * GELU_SCALE * (1.0 + 3.0 * GELU_CUBIC * pre_act * pre_act)
    return (value, slope)


def dot(a, b):
    return jnp.dot(a, b, preferred_element_type=F32)


def dot_nt(a, b):
    return lax.dot_general(a, b, (((1,), (1,)), ((), ())), preferred_element_type=F32)


def dot_tn(a, b):
    return lax.dot_general(a, b, (((0,), (0,)), ((), ())), preferred_element_type=F32)


def vmem_spec():
    return pl.BlockSpec(memory_space=pltpu.VMEM)


def head_kernel(tok_ref, cot_ref, up_left_ref, down_right_ref, both_ref, low_ref):
    rows = tok_ref.shape[0]
    tok, cot = tok_ref[...], cot_ref[...]
    both_ref[:rows] = tok
    both_ref[rows:] = cot
    low_ref[:rows] = dot(tok, up_left_ref[...]).astype(BF)
    low_ref[rows:] = dot_nt(cot, down_right_ref[...]).astype(BF)


def chosen(field, index_ref, level, block, rows, sub):
    ref, first_row = field
    pieces = []
    for j in range(2):
        column = pl.multiple_of(index_ref[level, block, j] * sub, sub)
        pieces.append(ref[pl.ds(first_row, rows), pl.ds(column, sub)])
    return jnp.concatenate(pieces, axis=1)


def spread(refs, rows):
    halves = []
    at = 0
    while at < len(refs):
        if refs[at].shape[0] == rows:
            halves.append(((refs[at], 0), (refs[at + 1], 0)))
            at += 2
        else:
            halves.append(((refs[at], 0), (refs[at], rows)))
            at += 1
    return halves


def middle_kernel(levels, fields_count, index_ref, *refs):
    rows = refs[0].shape[0]
    fields = spread(refs[:fields_count], rows)
    refs = refs[fields_count:]
    low_ref, up_ref, down_ref, up_right_ref, down_left_ref = refs[:5]
    act_ref, grad_ref, lowp_ref = refs[5:8]
    parts = spread(refs[8 : 8 + fields_count - 1], rows)
    out_acc, in_acc, low_acc = refs[8 + fields_count - 1 :]
    block = pl.program_id(0)
    sub = refs[8].shape[1] // 3

    @pl.when(block == 0)
    def _():
        out_acc[...] = jnp.zeros_like(out_acc)
        in_acc[...] = jnp.zeros_like(in_acc)
        low_acc[...] = jnp.zeros_like(low_acc)

    pre_act = dot(low_ref[:rows], up_right_ref[...])
    grad_hidden = dot_nt(low_ref[rows:], down_left_ref[...])
    for k in range(levels):
        pre_act += dot(chosen(fields[k][0], index_ref, k, block, rows, sub), up_ref[k])
        grad_hidden += dot_nt(chosen(fields[k][1], index_ref, k, block, rows, sub), down_ref[k])
    value, slope = gelu_parts(pre_act)
    act = value.astype(BF)
    grad = (grad_hidden * slope).astype(BF)
    act_ref[...] = act
    grad_ref[...] = grad
    low_acc[:rows] += dot(act, down_left_ref[...])
    low_acc[rows:] += dot_nt(grad, up_right_ref[...])
    for k in range(levels):
        out_pair = dot(act, down_ref[k])
        in_pair = dot_nt(grad, up_ref[k])
        for j in range(2):
            where = 3 * k + index_ref[k, block, j]
            out_acc[where] += out_pair[:, j * sub : (j + 1) * sub]
            in_acc[where] += in_pair[:, j * sub : (j + 1) * sub]

    @pl.when(block == pl.num_programs(0) - 1)
    def _():
        lowp_ref[...] = low_acc[...].astype(BF)
        for k in range(levels):
            for half, acc in zip(parts[k], (out_acc, in_acc)):
                ref, first = half
                for c in range(3):
                    ref[first : first + rows, c * sub : (c + 1) * sub] = acc[3 * k + c].astype(BF)


def grads_kernel(levels, groups, fields_count, index_ref, *refs):
    rows = refs[0].shape[0]
    fields = spread(refs[:fields_count], rows)
    low_ref, act_ref, grad_ref, out_ref = refs[fields_count:]
    block = pl.program_id(0)
    sub = refs[0].shape[1] // 3
    width = act_ref.shape[1]
    piece = width // groups
    per = 3 * piece
    up_base = (levels + 1) * per
    act_t = act_ref[...].T
    grad = grad_ref[...]
    for k in range(levels + 1):
        if k < levels:
            field = chosen(fields[k][0], index_ref, k, block, rows, sub)
            grad_field = chosen(fields[k][1], index_ref, k, block, rows, sub)
        else:
            field = low_ref[:rows]
            grad_field = low_ref[rows:]
        down = dot(act_t, grad_field).astype(BF)
        up = dot_tn(field, grad).astype(BF)
        for m in range(groups):
            slot = block * groups + m
            group = slot // 3
            row = pl.multiple_of(k * per + (slot - 3 * group) * piece, piece)
            out_ref[group, pl.ds(row, piece), :] = down[m * piece : (m + 1) * piece]
            row = pl.multiple_of(up_base + (block * (levels + 1) + k) * piece, piece)
            out_ref[m, pl.ds(row, piece), :] = up[m * piece : (m + 1) * piece]


def unpack_kernel(levels, sum_ref, down_ref, left_ref, up_ref, right_ref):
    per, width = left_ref.shape
    piece = right_ref.shape[0]
    for k in range(levels + 1):
        rows = sum_ref[k * per : (k + 1) * per]
        if k < levels:
            down_ref[k] = rows
        else:
            left_ref[...] = rows
        for block in range(right_ref.shape[1] // width):
            first = (levels + 1) * per + (block * (levels + 1) + k) * piece
            rows = sum_ref[first : first + piece]
            if k < levels:
                up_ref[k, :, block * width : (block + 1) * width] = rows
            else:
                right_ref[:, block * width : (block + 1) * width] = rows


def late_kernel(groups, both_ref, low_ref, out_ref):
    rows = low_ref.shape[0] // 2
    right = dot_tn(low_ref[:rows], both_ref[rows:]).astype(BF)
    left = dot_tn(both_ref[:rows], low_ref[rows:]).astype(BF)
    hr = right.shape[0] // groups
    hl = left.shape[0] // groups
    for m in range(groups):
        for c in range(right.shape[1] // 128):
            out_ref[m, c * hr : (c + 1) * hr] = right[m * hr : (m + 1) * hr, c * 128 : (c + 1) * 128]
        base = hr * (right.shape[1] // 128)
        for c in range(left.shape[1] // 128):
            out_ref[m, base + c * hl : base + (c + 1) * hl] = left[
                m * hl : (m + 1) * hl, c * 128 : (c + 1) * 128
            ]


def final_kernel(count, *refs):
    rows = refs[count].shape[0] // 2
    halves = spread(refs[:count], rows)
    low_ref, down_right_ref, up_left_ref, layer_ref, tokens_ref = refs[count:]
    for side, weight, out_ref in ((0, down_right_ref, layer_ref), (1, up_left_ref, tokens_ref)):
        total = None
        for half in halves:
            ref, first = half[side]
            value = ref[first : first + rows].astype(F32)
            total = value if total is None else total + value
        low = low_ref[side * rows : (side + 1) * rows]
        product = dot(low, weight[...]) if side == 0 else dot_nt(low, weight[...])
        out_ref[...] = (total + product).astype(BF)


def last_kernel(late_ref, right_ref, left_ref):
    late = late_ref[0].astype(F32)
    for m in range(1, late_ref.shape[0]):
        late += late_ref[m].astype(F32)
    late = late.astype(BF)
    hr, hl = right_ref.shape[0], left_ref.shape[0]
    for c in range(right_ref.shape[1] // 128):
        right_ref[:, c * 128 : (c + 1) * 128] = late[c * hr : (c + 1) * hr]
    base = hr * (right_ref.shape[1] // 128)
    for c in range(left_ref.shape[1] // 128):
        left_ref[:, c * 128 : (c + 1) * 128] = late[base + c * hl : base + (c + 1) * hl]


def params():
    return pltpu.CompilerParams(vmem_limit_bytes=VMEM_LIMIT)


def cost(flops, size):
    return pl.CostEstimate(flops=flops, bytes_accessed=size, transcendentals=0)


def group_exchange(pieces, groups):
    return lax.all_to_all(pieces, "hid", 0, 0, axis_index_groups=groups, tiled=True)


def group_scatter(value, groups):
    count = len(groups[0])
    pieces = value.reshape(count, value.shape[0] // count, value.shape[1])
    return jnp.sum(group_exchange(pieces, groups).astype(F32), axis=0).astype(BF)


def group_gather(value, groups):
    count = len(groups[0])
    pieces = jnp.broadcast_to(value[None], (count,) + value.shape)
    return group_exchange(pieces, groups).reshape(count * value.shape[0], value.shape[1])


def line_step(held, distance):
    count = lax.axis_size("hid")
    other = lax.ppermute(held, "hid", [(i, i ^ distance) for i in range(count)])
    return (held.astype(F32) + other.astype(F32)).astype(BF)


def hid_inner():
    return 8 if lax.axis_size("hid") % 8 == 0 else 1


def hid_columns():
    inner = hid_inner()
    return [list(range(i, lax.axis_size("hid"), inner)) for i in range(inner)]


def line_sum(held):
    trips = 1 + lax.shift_right_logical(lax.axis_index("hid"), 20)

    def once(_, value):
        step = 1
        while step < hid_inner():
            value = line_step(value, step)
            step *= 2
        return value

    return lax.fori_loop(0, trips, once, held)


def on_device(
    tokens, cotangent, up_tiles, down_tiles, block_index, up_left, up_right, down_left, down_right
):
    hid_count = lax.axis_size("hid")
    groups = lax.axis_size("tok")
    levels = hid_count.bit_length()
    rows, feat = tokens.shape
    blocks = block_index.shape[1]
    hidden = up_tiles.shape[2]
    width = hidden // blocks
    rank = up_left.shape[1]
    sub = feat // 3
    sds = jax.ShapeDtypeStruct

    def swap(value, distance):
        return lax.ppermute(value, "hid", [(i, i ^ distance) for i in range(hid_count)])

    tie = lax.optimization_barrier
    columns = hid_columns()
    tok_two = swap(tokens, 2)
    both, low_part = pl.pallas_call(
        head_kernel,
        out_shape=(sds((2 * rows, feat), BF), sds((2 * rows, rank), BF)),
        in_specs=[vmem_spec()] * 4,
        out_specs=(vmem_spec(), vmem_spec()),
        compiler_params=params(),
        cost_estimate=cost(4 * rows * feat * rank, 4 * rows * feat * 2),
        name="head",
    )(tokens, cotangent, up_left, down_right)
    total, both_x = tie((group_scatter(low_part, columns), both))
    x_one = swap(both_x, 8)
    x_two = swap(both_x, 16)
    total, x_one, x_two, tok_two, both_z, cot_z = tie(
        (line_sum(total), x_one, x_two, tok_two, both, cotangent)
    )
    tok_four = swap(tok_two, 6)
    cot_two = swap(cot_z, 2)
    z_one = swap(both_z, 1)
    low = group_gather(total, columns)
    cot_four = swap(cot_two, 6)
    fields = [tokens, cotangent, z_one, tok_two, cot_two, tok_four, cot_four, x_one, x_two]
    part_shapes = [(2 * rows, feat), (2 * rows, feat)]
    part_shapes += [(rows, feat)] * 4 + [(2 * rows, feat)] * 2

    def whole(shape):
        return pl.BlockSpec(shape, lambda b, *_: (0,) * len(shape))

    grid_params = pltpu.CompilerParams(
        dimension_semantics=("arbitrary",), vmem_limit_bytes=VMEM_LIMIT
    )
    flops = 2 * rows * (levels + 1) * 2 * sub * hidden
    middle = pl.pallas_call(
        functools.partial(middle_kernel, levels, len(fields)),
        grid_spec=pltpu.PrefetchScalarGridSpec(
            num_scalar_prefetch=1,
            grid=(blocks,),
            in_specs=[whole(field.shape) for field in fields]
            + [
                whole((2 * rows, rank)),
                pl.BlockSpec((levels, 2 * sub, width), lambda b, *_: (0, 0, b)),
                pl.BlockSpec((levels, width, 2 * sub), lambda b, *_: (0, b, 0)),
                pl.BlockSpec((rank, width), lambda b, *_: (0, b)),
                pl.BlockSpec((width, rank), lambda b, *_: (b, 0)),
            ],
            out_specs=[
                pl.BlockSpec((rows, width), lambda b, *_: (0, b)),
                pl.BlockSpec((rows, width), lambda b, *_: (0, b)),
                whole((2 * rows, rank)),
            ]
            + [whole(shape) for shape in part_shapes],
            scratch_shapes=[
                pltpu.VMEM((3 * levels, rows, sub), F32),
                pltpu.VMEM((3 * levels, rows, sub), F32),
                pltpu.VMEM((2 * rows, rank), F32),
            ],
        ),
        out_shape=[
            sds((rows, hidden), BF),
            sds((rows, hidden), BF),
            sds((2 * rows, rank), BF),
        ]
        + [sds(shape, BF) for shape in part_shapes],
        compiler_params=grid_params,
        cost_estimate=cost(4 * flops, 10 * 1024 * 1024),
        name="middle",
    )(block_index, *fields, low, up_tiles, down_tiles, up_right, down_left)
    act, grad_pre, lowp = middle[:3]
    parts = list(middle[3:])

    piece = width // groups
    chunk = 2 * (levels + 1) * 3 * piece
    packed = pl.pallas_call(
        functools.partial(grads_kernel, levels, groups, len(fields)),
        grid_spec=pltpu.PrefetchScalarGridSpec(
            num_scalar_prefetch=1,
            grid=(blocks,),
            in_specs=[whole(field.shape) for field in fields]
            + [
                whole((2 * rows, rank)),
                pl.BlockSpec((rows, width), lambda b, *_: (0, b)),
                pl.BlockSpec((rows, width), lambda b, *_: (0, b)),
            ],
            out_specs=whole((groups, chunk, width)),
        ),
        out_shape=sds((groups, chunk, width), BF),
        compiler_params=grid_params,
        cost_estimate=cost(2 * flops, 10 * 1024 * 1024),
        name="grads",
    )(block_index, *fields, low, act, grad_pre)

    own, one, out_two, in_two, out_four, in_four, x_one, x_two = parts
    out_four = swap(out_four, 6)
    total, x_one, x_two = tie((group_scatter(lowp, columns), x_one, x_two))
    x_one = swap(x_one, 8)
    x_two = swap(x_two, 16)
    total, x_one, x_two, out_four, in_four, one = tie(
        (line_sum(total), x_one, x_two, out_four, in_four, one)
    )

    def joined(first, second):
        return (first.astype(F32) + second.astype(F32)).astype(BF)

    in_four = swap(in_four, 6)
    out_two = swap(joined(out_two, out_four), 2)
    one = swap(one, 1)
    low2 = group_gather(total, columns)
    in_two = swap(joined(in_two, in_four), 2)
    parts = [own, one, out_two, in_two, x_one, x_two]
    summed = lax.psum_scatter(
        packed.reshape(groups * chunk, width), "tok", scatter_dimension=0, tiled=True
    )
    grad_down_tiles, grad_down_left, grad_up_tiles, grad_up_right = pl.pallas_call(
        functools.partial(unpack_kernel, levels),
        out_shape=(
            sds((levels, hidden // groups, 2 * sub), BF),
            sds((hidden // groups, rank), BF),
            sds((levels, 2 * sub // groups, hidden), BF),
            sds((rank // groups, hidden), BF),
        ),
        in_specs=[vmem_spec()],
        out_specs=(vmem_spec(),) * 4,
        compiler_params=params(),
        cost_estimate=cost(0, 4 * chunk * width),
        name="unpack",
    )(summed)

    late_rows = (rank // groups) * (feat // 128) + (feat // groups) * (rank // 128)
    late = pl.pallas_call(
        functools.partial(late_kernel, groups),
        out_shape=sds((groups, late_rows, 128), BF),
        in_specs=[vmem_spec()] * 2,
        out_specs=vmem_spec(),
        compiler_params=params(),
        cost_estimate=cost(4 * rows * feat * rank, 4 * rows * feat * 2),
        name="late",
    )(both, low2)
    late = lax.all_to_all(late, "tok", 0, 0, tiled=True)
    layer_out, grad_tokens = pl.pallas_call(
        functools.partial(final_kernel, len(parts)),
        out_shape=(sds((rows, feat), BF), sds((rows, feat), BF)),
        in_specs=[vmem_spec()] * (len(parts) + 3),
        out_specs=(vmem_spec(),) * 2,
        compiler_params=params(),
        cost_estimate=cost(4 * rows * feat * rank, 16 * rows * feat * 2),
        name="final",
    )(*parts, low2, down_right, up_left)
    grad_down_right, grad_up_left = pl.pallas_call(
        last_kernel,
        out_shape=(sds((rank // groups, feat), BF), sds((feat // groups, rank), BF)),
        in_specs=[vmem_spec()],
        out_specs=(vmem_spec(),) * 2,
        compiler_params=params(),
        cost_estimate=cost(rows * feat, 3 * rows * feat),
        name="last",
    )(late)
    return (
        layer_out,
        grad_tokens,
        grad_up_tiles,
        grad_down_tiles,
        grad_up_left,
        grad_up_right,
        grad_down_left,
        grad_down_right,
    )


def solution(mesh):
    return jax.shard_map(
        on_device,
        mesh=mesh,
        in_specs=(
            P("tok", "hid"),
            P("tok", "hid"),
            P(None, None, "hid"),
            P(None, "hid", None),
            P(None, "hid", None),
            P("hid", None),
            P(None, "hid"),
            P("hid", None),
            P(None, "hid"),
        ),
        out_specs=(
            P("tok", "hid"),
            P("tok", "hid"),
            P(None, "tok", "hid"),
            P(None, ("hid", "tok"), None),
            P(("hid", "tok"), None),
            P("tok", "hid"),
            P(("hid", "tok"), None),
            P("tok", "hid"),
        ),
        check_vma=False,
    )
```

```python
import functools

import jax
import jax.numpy as jnp
from jax import lax
from jax.experimental import pallas as pl
from jax.experimental.pallas import tpu as pltpu
from jax.sharding import PartitionSpec as P

GELU_SCALE = 0.7978845608028654
GELU_CUBIC = 0.044715
BF = jnp.bfloat16
F32 = jnp.float32
VMEM_LIMIT = 56 * 1024 * 1024


def gelu_parts(pre_act):
    inner = GELU_SCALE * (pre_act + GELU_CUBIC * pre_act * pre_act * pre_act)
    tanh_value = jnp.tanh(inner)
    value = 0.5 * pre_act * (1.0 + tanh_value)
    slope = 0.5 * (1.0 + tanh_value) + 0.5 * pre_act * (
        1.0 - tanh_value * tanh_value
    ) * GELU_SCALE * (1.0 + 3.0 * GELU_CUBIC * pre_act * pre_act)
    return (value, slope)


def dot(a, b):
    return jnp.dot(a, b, preferred_element_type=F32)


def dot_nt(a, b):
    return lax.dot_general(a, b, (((1,), (1,)), ((), ())), preferred_element_type=F32)


def dot_tn(a, b):
    return lax.dot_general(a, b, (((0,), (0,)), ((), ())), preferred_element_type=F32)


def vmem_spec():
    return pl.BlockSpec(memory_space=pltpu.VMEM)


def head_kernel(tok_ref, cot_ref, up_left_ref, down_right_ref, both_ref, low_ref):
    rows = tok_ref.shape[0]
    tok, cot = tok_ref[...], cot_ref[...]
    both_ref[:rows] = tok
    both_ref[rows:] = cot
    low_ref[:rows] = dot(tok, up_left_ref[...]).astype(BF)
    low_ref[rows:] = dot_nt(cot, down_right_ref[...]).astype(BF)


def chosen(ref, index_ref, level, block, first_row, rows, sub):
    pieces = []
    for j in range(2):
        column = pl.multiple_of(index_ref[level, block, j] * sub, sub)
        pieces.append(ref[pl.ds(first_row, rows), pl.ds(column, sub)])
    return jnp.concatenate(pieces, axis=1)


def middle_kernel(levels, index_ref, *refs):
    rows = refs[0].shape[0] // 2
    fields = refs[:levels]
    refs = refs[levels:]
    low_ref, up_ref, down_ref, up_right_ref, down_left_ref = refs[:5]
    act_ref, grad_ref, lowp_ref = refs[5:8]
    parts = refs[8 : 8 + levels]
    out_acc, in_acc, low_acc = refs[8 + levels :]
    block = pl.program_id(0)
    sub = refs[8].shape[1] // 3

    @pl.when(block == 0)
    def _():
        out_acc[...] = jnp.zeros_like(out_acc)
        in_acc[...] = jnp.zeros_like(in_acc)
        low_acc[...] = jnp.zeros_like(low_acc)

    pre_act = dot(low_ref[:rows], up_right_ref[...])
    grad_hidden = dot_nt(low_ref[rows:], down_left_ref[...])
    for k in range(levels):
        pre_act += dot(chosen(fields[k], index_ref, k, block, 0, rows, sub), up_ref[k])
        grad_hidden += dot_nt(chosen(fields[k], index_ref, k, block, rows, rows, sub), down_ref[k])
    value, slope = gelu_parts(pre_act)
    act = value.astype(BF)
    grad = (grad_hidden * slope).astype(BF)
    act_ref[...] = act
    grad_ref[...] = grad
    low_acc[:rows] += dot(act, down_left_ref[...])
    low_acc[rows:] += dot_nt(grad, up_right_ref[...])
    for k in range(levels):
        out_pair = dot(act, down_ref[k])
        in_pair = dot_nt(grad, up_ref[k])
        for j in range(2):
            where = 3 * k + index_ref[k, block, j]
            out_acc[where] += out_pair[:, j * sub : (j + 1) * sub]
            in_acc[where] += in_pair[:, j * sub : (j + 1) * sub]

    @pl.when(block == pl.num_programs(0) - 1)
    def _():
        lowp_ref[...] = low_acc[...].astype(BF)
        for k in range(levels):
            for c in range(3):
                columns = slice(c * sub, (c + 1) * sub)
                parts[k][:rows, columns] = out_acc[3 * k + c].astype(BF)
                parts[k][rows:, columns] = in_acc[3 * k + c].astype(BF)


def grads_kernel(levels, groups, index_ref, *refs):
    rows = refs[0].shape[0] // 2
    fields = refs[:levels]
    low_ref, act_ref, grad_ref, out_ref = refs[levels:]
    block = pl.program_id(0)
    sub = refs[0].shape[1] // 3
    width = act_ref.shape[1]
    piece = width // groups
    act_t = act_ref[...].T
    grad = grad_ref[...]
    for k in range(levels + 1):
        if k < levels:
            field = chosen(fields[k], index_ref, k, block, 0, rows, sub)
            grad_field = chosen(fields[k], index_ref, k, block, rows, rows, sub)
        else:
            field = low_ref[:rows]
            grad_field = low_ref[rows:]
        down = dot(act_t, grad_field).astype(BF)
        up = dot_tn(field, grad).astype(BF)
        for m in range(groups):
            slot = block * groups + m
            group = slot // 3
            row = pl.multiple_of((slot - 3 * group) * piece, piece)
            out_ref[group, k, 0, pl.ds(row, piece), :] = down[m * piece : (m + 1) * piece]
            row = pl.multiple_of(block * piece, piece)
            out_ref[m, k, 1, pl.ds(row, piece), :] = up[m * piece : (m + 1) * piece]


def unpack_kernel(sum_ref, down_ref, left_ref, up_ref, right_ref):
    levels = down_ref.shape[0]
    piece = right_ref.shape[0]
    width = sum_ref.shape[3]
    down_ref[...] = sum_ref[:levels, 0]
    left_ref[...] = sum_ref[levels, 0]
    for b in range(right_ref.shape[1] // width):
        columns = slice(b * width, (b + 1) * width)
        up_ref[:, :, columns] = sum_ref[:levels, 1, b * piece : (b + 1) * piece]
        right_ref[:, columns] = sum_ref[levels, 1, b * piece : (b + 1) * piece]


def late_kernel(groups, both_ref, low_ref, out_ref):
    rows = low_ref.shape[0] // 2
    right = dot_tn(low_ref[:rows], both_ref[rows:]).astype(BF)
    left = dot_tn(both_ref[:rows], low_ref[rows:]).astype(BF)
    hr = right.shape[0] // groups
    hl = left.shape[0] // groups
    for m in range(groups):
        for c in range(right.shape[1] // 128):
            out_ref[m, c * hr : (c + 1) * hr] = right[m * hr : (m + 1) * hr, c * 128 : (c + 1) * 128]
        base = hr * (right.shape[1] // 128)
        for c in range(left.shape[1] // 128):
            out_ref[m, base + c * hl : base + (c + 1) * hl] = left[
                m * hl : (m + 1) * hl, c * 128 : (c + 1) * 128
            ]


def final_kernel(count, *refs):
    parts = refs[:count]
    low_ref, down_right_ref, up_left_ref, layer_ref, tokens_ref = refs[count:]
    rows = low_ref.shape[0] // 2
    out = dot(low_ref[:rows], down_right_ref[...])
    back = dot_nt(low_ref[rows:], up_left_ref[...])
    for ref in parts:
        out += ref[:rows].astype(F32)
        back += ref[rows:].astype(F32)
    layer_ref[...] = out.astype(BF)
    tokens_ref[...] = back.astype(BF)


def last_kernel(late_ref, right_ref, left_ref):
    late = late_ref[0].astype(F32)
    for m in range(1, late_ref.shape[0]):
        late += late_ref[m].astype(F32)
    late = late.astype(BF)
    hr, hl = right_ref.shape[0], left_ref.shape[0]
    for c in range(right_ref.shape[1] // 128):
        right_ref[:, c * 128 : (c + 1) * 128] = late[c * hr : (c + 1) * hr]
    base = hr * (right_ref.shape[1] // 128)
    for c in range(left_ref.shape[1] // 128):
        left_ref[:, c * 128 : (c + 1) * 128] = late[base + c * hl : base + (c + 1) * hl]


def params():
    return pltpu.CompilerParams(vmem_limit_bytes=VMEM_LIMIT)


def cost(flops, size):
    return pl.CostEstimate(flops=flops, bytes_accessed=size, transcendentals=0)


def group_exchange(pieces, groups):
    return lax.all_to_all(pieces, "hid", 0, 0, axis_index_groups=groups, tiled=True)


def group_scatter(value, groups):
    count = len(groups[0])
    pieces = value.reshape(count, value.shape[0] // count, value.shape[1])
    return jnp.sum(group_exchange(pieces, groups).astype(F32), axis=0).astype(BF)


def group_gather(value, groups):
    count = len(groups[0])
    pieces = jnp.broadcast_to(value[None], (count,) + value.shape)
    return group_exchange(pieces, groups).reshape(count * value.shape[0], value.shape[1])


def line_step(held, distance):
    count = lax.axis_size("hid")
    other = lax.ppermute(held, "hid", [(i, i ^ distance) for i in range(count)])
    return (held.astype(F32) + other.astype(F32)).astype(BF)


def hid_inner():
    return 8 if lax.axis_size("hid") % 8 == 0 else 1


def hid_columns():
    inner = hid_inner()
    return [list(range(i, lax.axis_size("hid"), inner)) for i in range(inner)]


def fence(body, *operands):
    shapes = jax.eval_shape(body, *operands)

    def skipped(*_):
        return jax.tree.map(lambda leaf: jnp.zeros(leaf.shape, leaf.dtype), shapes)

    taken = lax.shift_right_logical(lax.axis_index("hid"), 20) == 0
    return lax.cond(taken, body, skipped, *operands)


def line_sum(held, steps):
    def body(value):
        for step in steps:
            value = line_step(value, step)
        return value

    return fence(body, held)


def on_device(
    tokens, cotangent, up_tiles, down_tiles, block_index, up_left, up_right, down_left, down_right
):
    hid_count = lax.axis_size("hid")
    groups = lax.axis_size("tok")
    levels = hid_count.bit_length()
    rows, feat = tokens.shape
    blocks = block_index.shape[1]
    hidden = up_tiles.shape[2]
    width = hidden // blocks
    rank = up_left.shape[1]
    sub = feat // 3
    sds = jax.ShapeDtypeStruct

    def swap(value, distance):
        return lax.ppermute(value, "hid", [(i, i ^ distance) for i in range(hid_count)])

    tie = lax.optimization_barrier
    columns = hid_columns()
    both, low_part = pl.pallas_call(
        head_kernel,
        out_shape=(sds((2 * rows, feat), BF), sds((2 * rows, rank), BF)),
        in_specs=[vmem_spec()] * 4,
        out_specs=(vmem_spec(), vmem_spec()),
        compiler_params=params(),
        cost_estimate=cost(4 * rows * feat * rank, 4 * rows * feat * 2),
        name="head",
    )(tokens, cotangent, up_left, down_right)
    z_two = swap(both, 2)
    total = group_scatter(low_part, columns)
    total, both_x = tie((total, both))
    x_one = swap(both_x, 8)
    x_two = swap(both_x, 16)
    total, z_two, x_one, x_two, both_z = tie(
        (line_sum(total, (6, 1, 2)), z_two, x_one, x_two, both)
    )
    z_four = swap(z_two, 6)
    z_one = swap(both_z, 1)
    low = group_gather(total, columns)
    fields = [both, z_one, z_two, z_four, x_one, x_two]
    part_shapes = [(2 * rows, feat)] * levels

    def whole(shape):
        return pl.BlockSpec(shape, lambda b, *_: (0,) * len(shape))

    grid_params = pltpu.CompilerParams(
        dimension_semantics=("arbitrary",), vmem_limit_bytes=VMEM_LIMIT
    )
    flops = 2 * rows * (levels + 1) * 2 * sub * hidden
    middle = pl.pallas_call(
        functools.partial(middle_kernel, levels),
        grid_spec=pltpu.PrefetchScalarGridSpec(
            num_scalar_prefetch=1,
            grid=(blocks,),
            in_specs=[whole(field.shape) for field in fields]
            + [
                whole((2 * rows, rank)),
                pl.BlockSpec((levels, 2 * sub, width), lambda b, *_: (0, 0, b)),
                pl.BlockSpec((levels, width, 2 * sub), lambda b, *_: (0, b, 0)),
                pl.BlockSpec((rank, width), lambda b, *_: (0, b)),
                pl.BlockSpec((width, rank), lambda b, *_: (b, 0)),
            ],
            out_specs=[
                pl.BlockSpec((rows, width), lambda b, *_: (0, b)),
                pl.BlockSpec((rows, width), lambda b, *_: (0, b)),
                whole((2 * rows, rank)),
            ]
            + [whole(shape) for shape in part_shapes],
            scratch_shapes=[
                pltpu.VMEM((3 * levels, rows, sub), F32),
                pltpu.VMEM((3 * levels, rows, sub), F32),
                pltpu.VMEM((2 * rows, rank), F32),
            ],
        ),
        out_shape=[
            sds((rows, hidden), BF),
            sds((rows, hidden), BF),
            sds((2 * rows, rank), BF),
        ]
        + [sds(shape, BF) for shape in part_shapes],
        compiler_params=grid_params,
        cost_estimate=cost(4 * flops, 10 * 1024 * 1024),
        name="middle",
    )(block_index, *fields, low, up_tiles, down_tiles, up_right, down_left)
    act, grad_pre, lowp = middle[:3]
    parts = list(middle[3:])

    piece = width // groups
    packed_shape = (groups, levels + 1, 2, 3 * piece, width)
    grads = pl.pallas_call(
        functools.partial(grads_kernel, levels, groups),
        grid_spec=pltpu.PrefetchScalarGridSpec(
            num_scalar_prefetch=1,
            grid=(blocks,),
            in_specs=[whole(field.shape) for field in fields]
            + [
                whole((2 * rows, rank)),
                pl.BlockSpec((rows, width), lambda b, *_: (0, b)),
                pl.BlockSpec((rows, width), lambda b, *_: (0, b)),
            ],
            out_specs=whole(packed_shape),
        ),
        out_shape=sds(packed_shape, BF),
        compiler_params=grid_params,
        cost_estimate=cost(2 * flops, 10 * 1024 * 1024),
        name="grads",
    )


    own, z_one, z_two, z_four, x_one, x_two = parts
    z_four = swap(z_four, 6)

    total = group_scatter(lowp, columns)
    packed = grads(block_index, *fields, low, act, grad_pre)
    total, packed = tie((total, packed))
    total, z_four, x_one, x_two, z_one = tie(
        (line_sum(total, (2, 1, 6)), z_four, x_one, x_two, z_one)
    )
    z_two = swap((z_two.astype(F32) + z_four.astype(F32)).astype(BF), 2)
    low2 = group_gather(total, columns)
    x_one = swap(x_one, 8)
    x_two = swap(x_two, 16)
    z_one = swap(z_one, 1)
    summed = lax.psum_scatter(
        packed.reshape(-1, width), "tok", scatter_dimension=0, tiled=True
    ).reshape(packed.shape[1:])
    grad_down_tiles, grad_down_left, grad_up_tiles, grad_up_right = pl.pallas_call(
        unpack_kernel,
        out_shape=(
            sds((levels, hidden // groups, 2 * sub), BF),
            sds((hidden // groups, rank), BF),
            sds((levels, 2 * sub // groups, hidden), BF),
            sds((rank // groups, hidden), BF),
        ),
        in_specs=[vmem_spec()],
        out_specs=(vmem_spec(),) * 4,
        compiler_params=params(),
        cost_estimate=cost(0, packed.size // 2),
        name="unpack",
    )(summed)

    late_rows = (rank // groups) * (feat // 128) + (feat // groups) * (rank // 128)
    late = pl.pallas_call(
        functools.partial(late_kernel, groups),
        out_shape=sds((groups, late_rows, 128), BF),
        in_specs=[vmem_spec()] * 2,
        out_specs=vmem_spec(),
        compiler_params=params(),
        cost_estimate=cost(4 * rows * feat * rank, 4 * rows * feat * 2),
        name="late",
    )

    moved = late(both, low2)
    moved = lax.all_to_all(moved, "tok", 0, 0, tiled=True)
    parts = (own, z_one, z_two, x_one, x_two)
    layer_out, grad_tokens = pl.pallas_call(
        functools.partial(final_kernel, len(parts)),
        out_shape=(sds((rows, feat), BF), sds((rows, feat), BF)),
        in_specs=[vmem_spec()] * (len(parts) + 3),
        out_specs=(vmem_spec(),) * 2,
        compiler_params=params(),
        cost_estimate=cost(4 * rows * feat * rank, 16 * rows * feat * 2),
        name="final",
    )(*parts, low2, down_right, up_left)
    grad_down_right, grad_up_left = pl.pallas_call(
        last_kernel,
        out_shape=(sds((rank // groups, feat), BF), sds((feat // groups, rank), BF)),
        in_specs=[vmem_spec()],
        out_specs=(vmem_spec(),) * 2,
        compiler_params=params(),
        cost_estimate=cost(rows * feat, 3 * rows * feat),
        name="last",
    )(moved)
    return (
        layer_out,
        grad_tokens,
        grad_up_tiles,
        grad_down_tiles,
        grad_up_left,
        grad_up_right,
        grad_down_left,
        grad_down_right,
    )


def solution(mesh):
    return jax.shard_map(
        on_device,
        mesh=mesh,
        in_specs=(
            P("tok", "hid"),
            P("tok", "hid"),
            P(None, None, "hid"),
            P(None, "hid", None),
            P(None, "hid", None),
            P("hid", None),
            P(None, "hid"),
            P("hid", None),
            P(None, "hid"),
        ),
        out_specs=(
            P("tok", "hid"),
            P("tok", "hid"),
            P(None, "tok", "hid"),
            P(None, ("hid", "tok"), None),
            P(("hid", "tok"), None),
            P("tok", "hid"),
            P(("hid", "tok"), None),
            P("tok", "hid"),
        ),
        check_vma=False,
    )
```

```python
import functools

import jax
import jax.numpy as jnp
from jax import lax
from jax.experimental import pallas as pl
from jax.experimental.pallas import tpu as pltpu
from jax.sharding import PartitionSpec as P

GELU_SCALE = 0.7978845608028654
GELU_CUBIC = 0.044715
BF = jnp.bfloat16
F32 = jnp.float32
VMEM_LIMIT = 16 * 1024 * 1024


def gelu_parts(pre_act):
    inner = GELU_SCALE * (pre_act + GELU_CUBIC * pre_act * pre_act * pre_act)
    tanh_value = jnp.tanh(inner)
    value = 0.5 * pre_act * (1.0 + tanh_value)
    slope = 0.5 * (1.0 + tanh_value) + 0.5 * pre_act * (
        1.0 - tanh_value * tanh_value
    ) * GELU_SCALE * (1.0 + 3.0 * GELU_CUBIC * pre_act * pre_act)
    return (value, slope)


def dot(a, b):
    return jnp.dot(a, b, preferred_element_type=F32)


def dot_nt(a, b):
    return lax.dot_general(a, b, (((1,), (1,)), ((), ())), preferred_element_type=F32)


def dot_tn(a, b):
    return lax.dot_general(a, b, (((0,), (0,)), ((), ())), preferred_element_type=F32)


def vmem_spec():
    return pl.BlockSpec(memory_space=pltpu.VMEM)


def head_kernel(tok_ref, cot_ref, up_left_ref, down_right_ref, both_ref, low_ref):
    rows = tok_ref.shape[0]
    tok, cot = tok_ref[...], cot_ref[...]
    both_ref[:rows] = tok
    both_ref[rows:] = cot
    low_ref[:rows] = dot(tok, up_left_ref[...]).astype(BF)
    low_ref[rows:] = dot_nt(cot, down_right_ref[...]).astype(BF)


def chosen(ref, index_ref, level, block, first_row, rows, sub):
    pieces = []
    for j in range(2):
        column = pl.multiple_of(index_ref[level, block, j] * sub, sub)
        pieces.append(ref[pl.ds(first_row, rows), pl.ds(column, sub)])
    return jnp.concatenate(pieces, axis=1)


def middle_kernel(levels, index_ref, *refs):
    rows = refs[0].shape[0] // 2
    fields = refs[:levels]
    refs = refs[levels:]
    low_ref, up_ref, down_ref, up_right_ref, down_left_ref = refs[:5]
    act_ref, grad_ref, lowp_ref = refs[5:8]
    parts = refs[8 : 8 + levels]
    out_acc, in_acc, low_acc = refs[8 + levels :]
    block = pl.program_id(0)
    sub = refs[8].shape[1] // 3

    @pl.when(block == 0)
    def _():
        out_acc[...] = jnp.zeros_like(out_acc)
        in_acc[...] = jnp.zeros_like(in_acc)
        low_acc[...] = jnp.zeros_like(low_acc)

    pre_act = dot(low_ref[:rows], up_right_ref[...])
    grad_hidden = dot_nt(low_ref[rows:], down_left_ref[...])
    for k in range(levels):
        pre_act += dot(chosen(fields[k], index_ref, k, block, 0, rows, sub), up_ref[k])
        grad_hidden += dot_nt(chosen(fields[k], index_ref, k, block, rows, rows, sub), down_ref[k])
    value, slope = gelu_parts(pre_act)
    act = value.astype(BF)
    grad = (grad_hidden * slope).astype(BF)
    act_ref[...] = act
    grad_ref[...] = grad
    low_acc[:rows] += dot(act, down_left_ref[...])
    low_acc[rows:] += dot_nt(grad, up_right_ref[...])
    for k in range(levels):
        out_pair = dot(act, down_ref[k])
        in_pair = dot_nt(grad, up_ref[k])
        for j in range(2):
            where = 3 * k + index_ref[k, block, j]
            out_acc[where] += out_pair[:, j * sub : (j + 1) * sub]
            in_acc[where] += in_pair[:, j * sub : (j + 1) * sub]

    @pl.when(block == pl.num_programs(0) - 1)
    def _():
        lowp_ref[...] = low_acc[...].astype(BF)
        for k in range(levels):
            for c in range(3):
                columns = slice(c * sub, (c + 1) * sub)
                parts[k][:rows, columns] = out_acc[3 * k + c].astype(BF)
                parts[k][rows:, columns] = in_acc[3 * k + c].astype(BF)


def grads_kernel(levels, groups, index_ref, *refs):
    rows = refs[0].shape[0] // 2
    fields = refs[:levels]
    low_ref, act_ref, grad_ref, out_ref = refs[levels:]
    block = pl.program_id(0)
    sub = refs[0].shape[1] // 3
    width = act_ref.shape[1]
    piece = width // groups
    act_t = act_ref[...].T
    grad = grad_ref[...]
    for k in range(levels + 1):
        if k < levels:
            field = chosen(fields[k], index_ref, k, block, 0, rows, sub)
            grad_field = chosen(fields[k], index_ref, k, block, rows, rows, sub)
        else:
            field = low_ref[:rows]
            grad_field = low_ref[rows:]
        down = dot(act_t, grad_field).astype(BF)
        up = dot_tn(field, grad).astype(BF)
        for m in range(groups):
            slot = block * groups + m
            group = slot // 3
            row = pl.multiple_of((slot - 3 * group) * piece, piece)
            out_ref[group, k, 0, pl.ds(row, piece), :] = down[m * piece : (m + 1) * piece]
            row = pl.multiple_of(block * piece, piece)
            out_ref[m, k, 1, pl.ds(row, piece), :] = up[m * piece : (m + 1) * piece]


def unpack_kernel(sum_ref, down_ref, left_ref, up_ref, right_ref):
    levels = down_ref.shape[0]
    piece = right_ref.shape[0]
    width = sum_ref.shape[3]
    down_ref[...] = sum_ref[:levels, 0]
    left_ref[...] = sum_ref[levels, 0]
    for b in range(right_ref.shape[1] // width):
        columns = slice(b * width, (b + 1) * width)
        up_ref[:, :, columns] = sum_ref[:levels, 1, b * piece : (b + 1) * piece]
        right_ref[:, columns] = sum_ref[levels, 1, b * piece : (b + 1) * piece]


def late_kernel(groups, both_ref, low_ref, out_ref):
    rows = low_ref.shape[0] // 2
    right = dot_tn(low_ref[:rows], both_ref[rows:]).astype(BF)
    left = dot_tn(both_ref[:rows], low_ref[rows:]).astype(BF)
    hr = right.shape[0] // groups
    hl = left.shape[0] // groups
    for m in range(groups):
        for c in range(right.shape[1] // 128):
            out_ref[m, c * hr : (c + 1) * hr] = right[m * hr : (m + 1) * hr, c * 128 : (c + 1) * 128]
        base = hr * (right.shape[1] // 128)
        for c in range(left.shape[1] // 128):
            out_ref[m, base + c * hl : base + (c + 1) * hl] = left[
                m * hl : (m + 1) * hl, c * 128 : (c + 1) * 128
            ]


def final_kernel(count, *refs):
    parts = refs[:count]
    low_ref, down_right_ref, up_left_ref, layer_ref, tokens_ref = refs[count:]
    rows = low_ref.shape[0] // 2
    out = dot(low_ref[:rows], down_right_ref[...])
    back = dot_nt(low_ref[rows:], up_left_ref[...])
    for ref in parts:
        out += ref[:rows].astype(F32)
        back += ref[rows:].astype(F32)
    layer_ref[...] = out.astype(BF)
    tokens_ref[...] = back.astype(BF)


def last_kernel(late_ref, right_ref, left_ref):
    late = late_ref[0].astype(F32)
    for m in range(1, late_ref.shape[0]):
        late += late_ref[m].astype(F32)
    late = late.astype(BF)
    hr, hl = right_ref.shape[0], left_ref.shape[0]
    for c in range(right_ref.shape[1] // 128):
        right_ref[:, c * 128 : (c + 1) * 128] = late[c * hr : (c + 1) * hr]
    base = hr * (right_ref.shape[1] // 128)
    for c in range(left_ref.shape[1] // 128):
        left_ref[:, c * 128 : (c + 1) * 128] = late[base + c * hl : base + (c + 1) * hl]


def params():
    return pltpu.CompilerParams(vmem_limit_bytes=VMEM_LIMIT)


def cost(flops, size):
    return pl.CostEstimate(flops=flops, bytes_accessed=size, transcendentals=0)


def group_exchange(pieces, groups):
    return lax.all_to_all(pieces, "hid", 0, 0, axis_index_groups=groups, tiled=True)


def group_scatter(value, groups):
    count = len(groups[0])
    pieces = value.reshape(count, value.shape[0] // count, value.shape[1])
    return jnp.sum(group_exchange(pieces, groups).astype(F32), axis=0).astype(BF)


def group_gather(value, groups):
    count = len(groups[0])
    pieces = jnp.broadcast_to(value[None], (count,) + value.shape)
    return group_exchange(pieces, groups).reshape(count * value.shape[0], value.shape[1])


def line_step(held, distance):
    count = lax.axis_size("hid")
    other = lax.ppermute(held, "hid", [(i, i ^ distance) for i in range(count)])
    return (held.astype(F32) + other.astype(F32)).astype(BF)


def hid_inner():
    return 8 if lax.axis_size("hid") % 8 == 0 else 1


def hid_columns():
    inner = hid_inner()
    return [list(range(i, lax.axis_size("hid"), inner)) for i in range(inner)]


def in_hbm(value):
    return pltpu.with_memory_space_constraint(value, pltpu.HBM)


def fence(body, *operands):
    shapes = jax.eval_shape(body, *operands)

    def skipped(*_):
        return jax.tree.map(lambda leaf: jnp.zeros(leaf.shape, leaf.dtype), shapes)

    taken = lax.shift_right_logical(lax.axis_index("hid"), 20) == 0
    return lax.cond(taken, body, skipped, *operands)


def line_sum(held, steps):
    def body(value):
        for step in steps:
            value = line_step(value, step)
        return value

    return fence(body, held)


def on_device(
    tokens, cotangent, up_tiles, down_tiles, block_index, up_left, up_right, down_left, down_right
):
    hid_count = lax.axis_size("hid")
    groups = lax.axis_size("tok")
    levels = hid_count.bit_length()
    rows, feat = tokens.shape
    blocks = block_index.shape[1]
    hidden = up_tiles.shape[2]
    width = hidden // blocks
    rank = up_left.shape[1]
    sub = feat // 3
    sds = jax.ShapeDtypeStruct

    def swap(value, distance):
        return lax.ppermute(value, "hid", [(i, i ^ distance) for i in range(hid_count)])

    tie = lax.optimization_barrier
    columns = hid_columns()
    both, low_part = pl.pallas_call(
        head_kernel,
        out_shape=(sds((2 * rows, feat), BF), sds((2 * rows, rank), BF)),
        in_specs=[vmem_spec()] * 4,
        out_specs=(vmem_spec(), vmem_spec()),
        compiler_params=params(),
        cost_estimate=cost(4 * rows * feat * rank, 4 * rows * feat * 2),
        name="head",
    )(tokens, cotangent, up_left, down_right)
    z_two = swap(both, 2)
    total = group_scatter(low_part, columns)
    total, both_x = tie((total, both))
    x_one = swap(both_x, 8)
    x_two = swap(both_x, 16)
    total, z_two, x_one, x_two, both_z = tie(
        (line_sum(total, (6, 1, 2)), z_two, x_one, x_two, both)
    )
    z_four = swap(z_two, 6)
    z_one = swap(both_z, 1)
    low = group_gather(total, columns)
    fields = [both, z_one, z_two, z_four, x_one, x_two]
    part_shapes = [(2 * rows, feat)] * levels

    def whole(shape):
        return pl.BlockSpec(shape, lambda b, *_: (0,) * len(shape))

    grid_params = pltpu.CompilerParams(
        dimension_semantics=("arbitrary",), vmem_limit_bytes=VMEM_LIMIT
    )
    flops = 2 * rows * (levels + 1) * 2 * sub * hidden
    middle = pl.pallas_call(
        functools.partial(middle_kernel, levels),
        grid_spec=pltpu.PrefetchScalarGridSpec(
            num_scalar_prefetch=1,
            grid=(blocks,),
            in_specs=[whole(field.shape) for field in fields]
            + [
                whole((2 * rows, rank)),
                pl.BlockSpec((levels, 2 * sub, width), lambda b, *_: (0, 0, b)),
                pl.BlockSpec((levels, width, 2 * sub), lambda b, *_: (0, b, 0)),
                pl.BlockSpec((rank, width), lambda b, *_: (0, b)),
                pl.BlockSpec((width, rank), lambda b, *_: (b, 0)),
            ],
            out_specs=[
                pl.BlockSpec((rows, width), lambda b, *_: (0, b)),
                pl.BlockSpec((rows, width), lambda b, *_: (0, b)),
                whole((2 * rows, rank)),
            ]
            + [whole(shape) for shape in part_shapes],
            scratch_shapes=[
                pltpu.VMEM((3 * levels, rows, sub), F32),
                pltpu.VMEM((3 * levels, rows, sub), F32),
                pltpu.VMEM((2 * rows, rank), F32),
            ],
        ),
        out_shape=[
            sds((rows, hidden), BF),
            sds((rows, hidden), BF),
            pltpu.HBM((2 * rows, rank), BF),
        ]
        + [pltpu.HBM(shape, BF) for shape in part_shapes],
        compiler_params=grid_params,
        cost_estimate=cost(4 * flops, 10 * 1024 * 1024),
        name="middle",
    )(block_index, *fields, low, *map(in_hbm, (up_tiles, down_tiles, up_right, down_left)))
    act, grad_pre, lowp = middle[:3]
    parts = list(middle[3:])

    piece = width // groups
    packed_shape = (groups, levels + 1, 2, 3 * piece, width)
    grads = pl.pallas_call(
        functools.partial(grads_kernel, levels, groups),
        grid_spec=pltpu.PrefetchScalarGridSpec(
            num_scalar_prefetch=1,
            grid=(blocks,),
            in_specs=[whole(field.shape) for field in fields]
            + [
                whole((2 * rows, rank)),
                pl.BlockSpec((rows, width), lambda b, *_: (0, b)),
                pl.BlockSpec((rows, width), lambda b, *_: (0, b)),
            ],
            out_specs=whole(packed_shape),
        ),
        out_shape=sds(packed_shape, BF),
        compiler_params=grid_params,
        cost_estimate=cost(2 * flops, 10 * 1024 * 1024),
        name="grads",
    )


    own, z_one, z_two, z_four, x_one, x_two = parts
    z_four = swap(z_four, 6)

    total = group_scatter(lowp, columns)
    packed = grads(block_index, *fields, low, act, grad_pre)
    total, packed = tie((total, packed))
    total, z_four, x_one, x_two, z_one = tie(
        (line_sum(total, (2, 1, 6)), z_four, x_one, x_two, z_one)
    )
    z_two = swap((z_two.astype(F32) + z_four.astype(F32)).astype(BF), 2)
    low2 = group_gather(total, columns)
    x_one = swap(x_one, 8)
    x_two = swap(x_two, 16)
    z_one = swap(z_one, 1)
    summed = lax.psum_scatter(
        packed.reshape(-1, width), "tok", scatter_dimension=0, tiled=True
    ).reshape(packed.shape[1:])
    grad_down_tiles, grad_down_left, grad_up_tiles, grad_up_right = pl.pallas_call(
        unpack_kernel,
        out_shape=(
            sds((levels, hidden // groups, 2 * sub), BF),
            sds((hidden // groups, rank), BF),
            sds((levels, 2 * sub // groups, hidden), BF),
            sds((rank // groups, hidden), BF),
        ),
        in_specs=[vmem_spec()],
        out_specs=(vmem_spec(),) * 4,
        compiler_params=params(),
        cost_estimate=cost(0, packed.size // 2),
        name="unpack",
    )(summed)

    late_rows = (rank // groups) * (feat // 128) + (feat // groups) * (rank // 128)
    late = pl.pallas_call(
        functools.partial(late_kernel, groups),
        out_shape=sds((groups, late_rows, 128), BF),
        in_specs=[vmem_spec()] * 2,
        out_specs=vmem_spec(),
        compiler_params=params(),
        cost_estimate=cost(4 * rows * feat * rank, 4 * rows * feat * 2),
        name="late",
    )

    moved = late(both, low2)
    moved = lax.all_to_all(moved, "tok", 0, 0, tiled=True)
    x_two, grad_down_tiles, grad_up_tiles = tie((x_two, grad_down_tiles, grad_up_tiles))
    parts = (own, z_one, z_two, x_one, x_two)
    layer_out, grad_tokens = pl.pallas_call(
        functools.partial(final_kernel, len(parts)),
        out_shape=(sds((rows, feat), BF), sds((rows, feat), BF)),
        in_specs=[vmem_spec()] * (len(parts) + 3),
        out_specs=(vmem_spec(),) * 2,
        compiler_params=params(),
        cost_estimate=cost(4 * rows * feat * rank, 16 * rows * feat * 2),
        name="final",
    )(*parts, low2, down_right, up_left)
    moved, layer_out = tie((moved, layer_out))
    grad_down_right, grad_up_left = pl.pallas_call(
        last_kernel,
        out_shape=(sds((rank // groups, feat), BF), sds((feat // groups, rank), BF)),
        in_specs=[vmem_spec()],
        out_specs=(vmem_spec(),) * 2,
        compiler_params=params(),
        cost_estimate=cost(rows * feat, 3 * rows * feat),
        name="last",
    )(moved)
    return (
        layer_out,
        grad_tokens,
        grad_up_tiles,
        grad_down_tiles,
        grad_up_left,
        grad_up_right,
        grad_down_left,
        grad_down_right,
    )


def solution(mesh):
    return jax.shard_map(
        on_device,
        mesh=mesh,
        in_specs=(
            P("tok", "hid"),
            P("tok", "hid"),
            P(None, None, "hid"),
            P(None, "hid", None),
            P(None, "hid", None),
            P("hid", None),
            P(None, "hid"),
            P("hid", None),
            P(None, "hid"),
        ),
        out_specs=(
            P("tok", "hid"),
            P("tok", "hid"),
            P(None, "tok", "hid"),
            P(None, ("hid", "tok"), None),
            P(("hid", "tok"), None),
            P("tok", "hid"),
            P(("hid", "tok"), None),
            P("tok", "hid"),
        ),
        check_vma=False,
    )
```

```python
import functools

import jax
import jax.numpy as jnp
from jax import lax
from jax.experimental import pallas as pl
from jax.experimental.pallas import tpu as pltpu
from jax.sharding import PartitionSpec as P

GELU_SCALE = 0.7978845608028654
GELU_CUBIC = 0.044715
BF = jnp.bfloat16
F32 = jnp.float32
VMEM_LIMIT = 16 * 1024 * 1024


def gelu_parts(pre_act):
    inner = GELU_SCALE * (pre_act + GELU_CUBIC * pre_act * pre_act * pre_act)
    tanh_value = jnp.tanh(inner)
    value = 0.5 * pre_act * (1.0 + tanh_value)
    slope = 0.5 * (1.0 + tanh_value) + 0.5 * pre_act * (
        1.0 - tanh_value * tanh_value
    ) * GELU_SCALE * (1.0 + 3.0 * GELU_CUBIC * pre_act * pre_act)
    return (value, slope)


def dot(a, b):
    return jnp.dot(a, b, preferred_element_type=F32)


def dot_nt(a, b):
    return lax.dot_general(a, b, (((1,), (1,)), ((), ())), preferred_element_type=F32)


def dot_tn(a, b):
    return lax.dot_general(a, b, (((0,), (0,)), ((), ())), preferred_element_type=F32)


def vmem_spec():
    return pl.BlockSpec(memory_space=pltpu.VMEM)


def head_kernel(tok_ref, cot_ref, up_left_ref, down_right_ref, both_ref, low_ref):
    rows = tok_ref.shape[0]
    tok, cot = tok_ref[...], cot_ref[...]
    both_ref[:rows] = tok
    both_ref[rows:] = cot
    low_ref[:rows] = dot(tok, up_left_ref[...]).astype(BF)
    low_ref[rows:] = dot_nt(cot, down_right_ref[...]).astype(BF)


def chosen(ref, index_ref, level, block, first_row, rows, sub):
    pieces = []
    for j in range(2):
        column = pl.multiple_of(index_ref[level, block, j] * sub, sub)
        pieces.append(ref[pl.ds(first_row, rows), pl.ds(column, sub)])
    return jnp.concatenate(pieces, axis=1)


def middle_kernel(levels, index_ref, *refs):
    rows = refs[0].shape[0] // 2
    fields = refs[:levels]
    refs = refs[levels:]
    low_ref, up_ref, down_ref, up_right_ref, down_left_ref = refs[:5]
    act_ref, grad_ref, lowp_ref = refs[5:8]
    parts = refs[8 : 8 + levels]
    out_acc, in_acc, low_acc = refs[8 + levels :]
    block = pl.program_id(0)
    sub = refs[8].shape[1] // 3

    @pl.when(block == 0)
    def _():
        out_acc[...] = jnp.zeros_like(out_acc)
        in_acc[...] = jnp.zeros_like(in_acc)
        low_acc[...] = jnp.zeros_like(low_acc)

    pre_act = dot(low_ref[:rows], up_right_ref[...])
    grad_hidden = dot_nt(low_ref[rows:], down_left_ref[...])
    for k in range(levels):
        pre_act += dot(chosen(fields[k], index_ref, k, block, 0, rows, sub), up_ref[k])
        grad_hidden += dot_nt(chosen(fields[k], index_ref, k, block, rows, rows, sub), down_ref[k])
    value, slope = gelu_parts(pre_act)
    act = value.astype(BF)
    grad = (grad_hidden * slope).astype(BF)
    act_ref[...] = act
    grad_ref[...] = grad
    low_acc[:rows] += dot(act, down_left_ref[...])
    low_acc[rows:] += dot_nt(grad, up_right_ref[...])
    for k in range(levels):
        out_pair = dot(act, down_ref[k])
        in_pair = dot_nt(grad, up_ref[k])
        for j in range(2):
            where = 3 * k + index_ref[k, block, j]
            out_acc[where] += out_pair[:, j * sub : (j + 1) * sub]
            in_acc[where] += in_pair[:, j * sub : (j + 1) * sub]

    @pl.when(block == pl.num_programs(0) - 1)
    def _():
        lowp_ref[...] = low_acc[...].astype(BF)
        for k in range(levels):
            for c in range(3):
                columns = slice(c * sub, (c + 1) * sub)
                parts[k][:rows, columns] = out_acc[3 * k + c].astype(BF)
                parts[k][rows:, columns] = in_acc[3 * k + c].astype(BF)


def grads_kernel(levels, groups, index_ref, *refs):
    rows = refs[0].shape[0] // 2
    fields = refs[:levels]
    low_ref, act_ref, grad_ref, out_ref = refs[levels:]
    block = pl.program_id(0)
    sub = refs[0].shape[1] // 3
    width = act_ref.shape[1]
    piece = width // groups
    act_t = act_ref[...].T
    grad = grad_ref[...]
    for k in range(levels + 1):
        if k < levels:
            field = chosen(fields[k], index_ref, k, block, 0, rows, sub)
            grad_field = chosen(fields[k], index_ref, k, block, rows, rows, sub)
        else:
            field = low_ref[:rows]
            grad_field = low_ref[rows:]
        down = dot(act_t, grad_field).astype(BF)
        up = dot_tn(field, grad).astype(BF)
        for m in range(groups):
            slot = block * groups + m
            group = slot // 3
            row = pl.multiple_of((slot - 3 * group) * piece, piece)
            out_ref[group, k, 0, pl.ds(row, piece), :] = down[m * piece : (m + 1) * piece]
            row = pl.multiple_of(block * piece, piece)
            out_ref[m, k, 1, pl.ds(row, piece), :] = up[m * piece : (m + 1) * piece]


def unpack_kernel(sum_ref, down_ref, left_ref, up_ref, right_ref):
    levels = down_ref.shape[0]
    piece = right_ref.shape[0]
    width = sum_ref.shape[3]
    down_ref[...] = sum_ref[:levels, 0]
    left_ref[...] = sum_ref[levels, 0]
    for b in range(right_ref.shape[1] // width):
        columns = slice(b * width, (b + 1) * width)
        up_ref[:, :, columns] = sum_ref[:levels, 1, b * piece : (b + 1) * piece]
        right_ref[:, columns] = sum_ref[levels, 1, b * piece : (b + 1) * piece]


def late_kernel(groups, both_ref, *refs):
    *pieces, out_ref, low_ref = refs
    assemble(low_ref, pieces)
    rows = low_ref.shape[0] // 2
    right = dot_tn(low_ref[:rows], both_ref[rows:]).astype(BF)
    left = dot_tn(both_ref[:rows], low_ref[rows:]).astype(BF)
    hr = right.shape[0] // groups
    hl = left.shape[0] // groups
    for m in range(groups):
        for c in range(right.shape[1] // 128):
            out_ref[m, c * hr : (c + 1) * hr] = right[m * hr : (m + 1) * hr, c * 128 : (c + 1) * 128]
        base = hr * (right.shape[1] // 128)
        for c in range(left.shape[1] // 128):
            out_ref[m, base + c * hl : base + (c + 1) * hl] = left[
                m * hl : (m + 1) * hl, c * 128 : (c + 1) * 128
            ]


def final_kernel(count, *refs):
    parts = refs[:count]
    low_ref, down_right_ref, up_left_ref, layer_ref, tokens_ref = refs[count:]
    rows = low_ref.shape[0] // 2
    out = dot(low_ref[:rows], down_right_ref[...])
    back = dot_nt(low_ref[rows:], up_left_ref[...])
    for ref in parts:
        out += ref[:rows].astype(F32)
        back += ref[rows:].astype(F32)
    layer_ref[...] = out.astype(BF)
    tokens_ref[...] = back.astype(BF)


def last_kernel(late_ref, right_ref, left_ref):
    late = late_ref[0].astype(F32)
    for m in range(1, late_ref.shape[0]):
        late += late_ref[m].astype(F32)
    late = late.astype(BF)
    hr, hl = right_ref.shape[0], left_ref.shape[0]
    for c in range(right_ref.shape[1] // 128):
        right_ref[:, c * 128 : (c + 1) * 128] = late[c * hr : (c + 1) * hr]
    base = hr * (right_ref.shape[1] // 128)
    for c in range(left_ref.shape[1] // 128):
        left_ref[:, c * 128 : (c + 1) * 128] = late[base + c * hl : base + (c + 1) * hl]


def params():
    return pltpu.CompilerParams(vmem_limit_bytes=VMEM_LIMIT)


def cost(flops, size):
    return pl.CostEstimate(flops=flops, bytes_accessed=size, transcendentals=0)


def group_exchange(pieces, groups):
    return lax.all_to_all(pieces, "hid", 0, 0, axis_index_groups=groups, tiled=True)


def group_scatter(value, groups, beside=None):
    count = len(groups[0])
    pieces = value.reshape(count, value.shape[0] // count, value.shape[1])
    pieces = group_exchange(pieces, groups)
    if beside is not None:
        pieces, beside = lax.optimization_barrier((pieces, beside))
    return jnp.sum(pieces.astype(F32), axis=0).astype(BF), beside


def group_gather(value, groups):
    count = len(groups[0])
    pieces = jnp.broadcast_to(value[None], (count,) + value.shape)
    return group_exchange(pieces, groups).reshape(count * value.shape[0], value.shape[1])


def outer_shift(value, step):
    count, inner = lax.axis_size("hid"), hid_inner()
    return lax.ppermute(value, "hid", [(i, (i + step * inner) % count) for i in range(count)])


def outer_pieces(value):
    return [value] + [outer_shift(value, d) for d in range(1, len(hid_columns()[0]))]


def assemble(out_ref, piece_refs):
    count, tall = len(piece_refs), piece_refs[0].shape[0]
    place = lax.axis_index("hid") // hid_inner()
    for d, ref in enumerate(piece_refs):
        first = pl.multiple_of(lax.rem(place + count - d, count) * tall, tall)
        out_ref[pl.ds(first, tall), :] = ref[...]


def line_step(held, distance):
    count = lax.axis_size("hid")
    other = lax.ppermute(held, "hid", [(i, i ^ distance) for i in range(count)])
    return (held.astype(F32) + other.astype(F32)).astype(BF)


def hid_inner():
    return 8 if lax.axis_size("hid") % 8 == 0 else 1


def hid_columns():
    inner = hid_inner()
    return [list(range(i, lax.axis_size("hid"), inner)) for i in range(inner)]


def in_hbm(value):
    return pltpu.with_memory_space_constraint(value, pltpu.HBM)


def fence(body, *operands):
    shapes = jax.eval_shape(body, *operands)

    def skipped(*_):
        return jax.tree.map(lambda leaf: jnp.zeros(leaf.shape, leaf.dtype), shapes)

    taken = lax.shift_right_logical(lax.axis_index("hid"), 20) == 0
    return lax.cond(taken, body, skipped, *operands)


def line_sum(held, steps):
    def body(value):
        for step in steps:
            value = line_step(value, step)
        return value

    return fence(body, held)


def on_device(
    tokens, cotangent, up_tiles, down_tiles, block_index, up_left, up_right, down_left, down_right
):
    hid_count = lax.axis_size("hid")
    groups = lax.axis_size("tok")
    levels = hid_count.bit_length()
    rows, feat = tokens.shape
    blocks = block_index.shape[1]
    hidden = up_tiles.shape[2]
    width = hidden // blocks
    rank = up_left.shape[1]
    sub = feat // 3
    sds = jax.ShapeDtypeStruct

    def swap(value, distance):
        return lax.ppermute(value, "hid", [(i, i ^ distance) for i in range(hid_count)])

    tie = lax.optimization_barrier
    columns = hid_columns()
    both, low_part = pl.pallas_call(
        head_kernel,
        out_shape=(sds((2 * rows, feat), BF), sds((2 * rows, rank), BF)),
        in_specs=[vmem_spec()] * 4,
        out_specs=(vmem_spec(), vmem_spec()),
        compiler_params=params(),
        cost_estimate=cost(4 * rows * feat * rank, 4 * rows * feat * 2),
        name="head",
    )(tokens, cotangent, up_left, down_right)
    z_two = swap(both, 2)
    total, _ = group_scatter(low_part, columns)
    total, both_x = tie((total, both))
    x_one = swap(both_x, 8)
    x_two = swap(both_x, 16)
    total, z_two, x_one, x_two, both_z = tie(
        (line_sum(total, (1, 6, 2)), z_two, x_one, x_two, both)
    )
    z_four = swap(z_two, 6)
    z_one = swap(both_z, 1)
    low = group_gather(total, columns)
    fields = [both, z_one, z_two, z_four, x_one, x_two]
    part_shapes = [(2 * rows, feat)] * levels

    def whole(shape):
        return pl.BlockSpec(shape, lambda b, *_: (0,) * len(shape))

    grid_params = pltpu.CompilerParams(
        dimension_semantics=("arbitrary",), vmem_limit_bytes=VMEM_LIMIT
    )
    flops = 2 * rows * (levels + 1) * 2 * sub * hidden
    middle = pl.pallas_call(
        functools.partial(middle_kernel, levels),
        grid_spec=pltpu.PrefetchScalarGridSpec(
            num_scalar_prefetch=1,
            grid=(blocks,),
            in_specs=[whole(field.shape) for field in fields]
            + [
                whole((2 * rows, rank)),
                pl.BlockSpec((levels, 2 * sub, width), lambda b, *_: (0, 0, b)),
                pl.BlockSpec((levels, width, 2 * sub), lambda b, *_: (0, b, 0)),
                pl.BlockSpec((rank, width), lambda b, *_: (0, b)),
                pl.BlockSpec((width, rank), lambda b, *_: (b, 0)),
            ],
            out_specs=[
                pl.BlockSpec((rows, width), lambda b, *_: (0, b)),
                pl.BlockSpec((rows, width), lambda b, *_: (0, b)),
                whole((2 * rows, rank)),
            ]
            + [whole(shape) for shape in part_shapes],
            scratch_shapes=[
                pltpu.VMEM((3 * levels, rows, sub), F32),
                pltpu.VMEM((3 * levels, rows, sub), F32),
                pltpu.VMEM((2 * rows, rank), F32),
            ],
        ),
        out_shape=[
            sds((rows, hidden), BF),
            sds((rows, hidden), BF),
            pltpu.HBM((2 * rows, rank), BF),
        ]
        + [pltpu.HBM(shape, BF) for shape in part_shapes],
        compiler_params=grid_params,
        cost_estimate=cost(4 * flops, 10 * 1024 * 1024),
        name="middle",
    )(block_index, *fields, low, *map(in_hbm, (up_tiles, down_tiles, up_right, down_left)))
    act, grad_pre, lowp = middle[:3]
    parts = list(middle[3:])

    piece = width // groups
    packed_shape = (groups, levels + 1, 2, 3 * piece, width)
    grads = pl.pallas_call(
        functools.partial(grads_kernel, levels, groups),
        grid_spec=pltpu.PrefetchScalarGridSpec(
            num_scalar_prefetch=1,
            grid=(blocks,),
            in_specs=[whole(field.shape) for field in fields]
            + [
                whole((2 * rows, rank)),
                pl.BlockSpec((rows, width), lambda b, *_: (0, b)),
                pl.BlockSpec((rows, width), lambda b, *_: (0, b)),
            ],
            out_specs=whole(packed_shape),
        ),
        out_shape=sds(packed_shape, BF),
        compiler_params=grid_params,
        cost_estimate=cost(2 * flops, 10 * 1024 * 1024),
        name="grads",
    )


    own, z_one, z_two, z_four, x_one, x_two = parts
    z_four = swap(z_four, 6)

    packed = grads(block_index, *fields, low, act, grad_pre)
    total, packed = group_scatter(lowp, columns, packed)
    total, z_four, x_one, x_two, z_one = tie(
        (line_sum(total, (2, 1, 6)), z_four, x_one, x_two, z_one)
    )
    z_two = swap((z_two.astype(F32) + z_four.astype(F32)).astype(BF), 2)
    low_pieces = outer_pieces(total)
    x_one = swap(x_one, 8)
    x_two = swap(x_two, 16)
    z_one = swap(z_one, 1)
    summed = lax.psum_scatter(
        packed.reshape(-1, width), "tok", scatter_dimension=0, tiled=True
    ).reshape(packed.shape[1:])
    grad_down_tiles, grad_down_left, grad_up_tiles, grad_up_right = pl.pallas_call(
        unpack_kernel,
        out_shape=(
            sds((levels, hidden // groups, 2 * sub), BF),
            sds((hidden // groups, rank), BF),
            sds((levels, 2 * sub // groups, hidden), BF),
            sds((rank // groups, hidden), BF),
        ),
        in_specs=[vmem_spec()],
        out_specs=(vmem_spec(),) * 4,
        compiler_params=params(),
        cost_estimate=cost(0, packed.size // 2),
        name="unpack",
    )(summed)

    late_rows = (rank // groups) * (feat // 128) + (feat // groups) * (rank // 128)
    late = pl.pallas_call(
        functools.partial(late_kernel, groups),
        out_shape=(sds((groups, late_rows, 128), BF), sds((2 * rows, rank), BF)),
        in_specs=[vmem_spec()] * (1 + len(low_pieces)),
        out_specs=(vmem_spec(),) * 2,
        compiler_params=params(),
        cost_estimate=cost(4 * rows * feat * rank, 4 * rows * feat * 2),
        name="late",
    )

    moved, low2 = late(both, *low_pieces)
    moved = lax.all_to_all(moved, "tok", 0, 0, tiled=True)
    x_two, grad_down_tiles, grad_up_tiles = tie((x_two, grad_down_tiles, grad_up_tiles))
    parts = (own, z_one, z_two, x_one, x_two)
    layer_out, grad_tokens = pl.pallas_call(
        functools.partial(final_kernel, len(parts)),
        out_shape=(sds((rows, feat), BF), sds((rows, feat), BF)),
        in_specs=[vmem_spec()] * (len(parts) + 3),
        out_specs=(vmem_spec(),) * 2,
        compiler_params=params(),
        cost_estimate=cost(4 * rows * feat * rank, 16 * rows * feat * 2),
        name="final",
    )(*parts, low2, down_right, up_left)
    moved, layer_out = tie((moved, layer_out))
    grad_down_right, grad_up_left = pl.pallas_call(
        last_kernel,
        out_shape=(sds((rank // groups, feat), BF), sds((feat // groups, rank), BF)),
        in_specs=[vmem_spec()],
        out_specs=(vmem_spec(),) * 2,
        compiler_params=params(),
        cost_estimate=cost(rows * feat, 3 * rows * feat),
        name="last",
    )(moved)
    return (
        layer_out,
        grad_tokens,
        grad_up_tiles,
        grad_down_tiles,
        grad_up_left,
        grad_up_right,
        grad_down_left,
        grad_down_right,
    )


def solution(mesh):
    return jax.shard_map(
        on_device,
        mesh=mesh,
        in_specs=(
            P("tok", "hid"),
            P("tok", "hid"),
            P(None, None, "hid"),
            P(None, "hid", None),
            P(None, "hid", None),
            P("hid", None),
            P(None, "hid"),
            P("hid", None),
            P(None, "hid"),
        ),
        out_specs=(
            P("tok", "hid"),
            P("tok", "hid"),
            P(None, "tok", "hid"),
            P(None, ("hid", "tok"), None),
            P(("hid", "tok"), None),
            P("tok", "hid"),
            P(("hid", "tok"), None),
            P("tok", "hid"),
        ),
        check_vma=False,
    )
```

```python
import functools

import jax
import jax.numpy as jnp
from jax import lax
from jax.experimental import pallas as pl
from jax.experimental.pallas import tpu as pltpu
from jax.sharding import PartitionSpec as P

GELU_SCALE = 0.7978845608028654
GELU_CUBIC = 0.044715
BF = jnp.bfloat16
F32 = jnp.float32
VMEM_LIMIT = 16 * 1024 * 1024


def gelu_parts(pre_act):
    inner = GELU_SCALE * (pre_act + GELU_CUBIC * pre_act * pre_act * pre_act)
    tanh_value = jnp.tanh(inner)
    value = 0.5 * pre_act * (1.0 + tanh_value)
    slope = 0.5 * (1.0 + tanh_value) + 0.5 * pre_act * (
        1.0 - tanh_value * tanh_value
    ) * GELU_SCALE * (1.0 + 3.0 * GELU_CUBIC * pre_act * pre_act)
    return (value, slope)


def dot(a, b):
    return jnp.dot(a, b, preferred_element_type=F32)


def dot_nt(a, b):
    return lax.dot_general(a, b, (((1,), (1,)), ((), ())), preferred_element_type=F32)


def dot_tn(a, b):
    return lax.dot_general(a, b, (((0,), (0,)), ((), ())), preferred_element_type=F32)


def vmem_spec():
    return pl.BlockSpec(memory_space=pltpu.VMEM)


def head_kernel(tok_ref, cot_ref, up_left_ref, down_right_ref, both_ref, low_ref):
    rows = tok_ref.shape[0]
    tok, cot = tok_ref[...], cot_ref[...]
    both_ref[:rows] = tok
    both_ref[rows:] = cot
    low_ref[:rows] = dot(tok, up_left_ref[...]).astype(BF)
    low_ref[rows:] = dot_nt(cot, down_right_ref[...]).astype(BF)


def chosen(ref, index_ref, level, block, first_row, rows, sub):
    pieces = []
    for j in range(2):
        column = pl.multiple_of(index_ref[level, block, j] * sub, sub)
        pieces.append(ref[pl.ds(first_row, rows), pl.ds(column, sub)])
    return jnp.concatenate(pieces, axis=1)


def middle_kernel(levels, index_ref, *refs):
    rows = refs[0].shape[0] // 2
    fields = refs[:levels]
    refs = refs[levels:]
    low_ref, up_ref, down_ref, up_right_ref, down_left_ref = refs[:5]
    act_ref, grad_ref, lowp_ref = refs[5:8]
    parts = refs[8 : 8 + levels]
    out_acc, in_acc, low_acc = refs[8 + levels :]
    block = pl.program_id(0)
    sub = refs[8].shape[1] // 3

    @pl.when(block == 0)
    def _():
        out_acc[...] = jnp.zeros_like(out_acc)
        in_acc[...] = jnp.zeros_like(in_acc)
        low_acc[...] = jnp.zeros_like(low_acc)

    pre_act = dot(low_ref[:rows], up_right_ref[...])
    grad_hidden = dot_nt(low_ref[rows:], down_left_ref[...])
    for k in range(levels):
        pre_act += dot(chosen(fields[k], index_ref, k, block, 0, rows, sub), up_ref[k])
        grad_hidden += dot_nt(chosen(fields[k], index_ref, k, block, rows, rows, sub), down_ref[k])
    value, slope = gelu_parts(pre_act)
    act = value.astype(BF)
    grad = (grad_hidden * slope).astype(BF)
    act_ref[...] = act
    grad_ref[...] = grad
    low_acc[:rows] += dot(act, down_left_ref[...])
    low_acc[rows:] += dot_nt(grad, up_right_ref[...])
    for k in range(levels):
        out_pair = dot(act, down_ref[k])
        in_pair = dot_nt(grad, up_ref[k])
        for j in range(2):
            where = 3 * k + index_ref[k, block, j]
            out_acc[where] += out_pair[:, j * sub : (j + 1) * sub]
            in_acc[where] += in_pair[:, j * sub : (j + 1) * sub]

    @pl.when(block == pl.num_programs(0) - 1)
    def _():
        lowp_ref[...] = low_acc[...].astype(BF)
        for k in range(levels):
            for c in range(3):
                columns = slice(c * sub, (c + 1) * sub)
                parts[k][:rows, columns] = out_acc[3 * k + c].astype(BF)
                parts[k][rows:, columns] = in_acc[3 * k + c].astype(BF)


def grads_kernel(levels, groups, index_ref, *refs):
    rows = refs[0].shape[0] // 2
    fields = refs[:levels]
    low_ref, act_ref, grad_ref, out_ref = refs[levels:]
    block = pl.program_id(0)
    sub = refs[0].shape[1] // 3
    width = act_ref.shape[1]
    piece = width // groups
    act_t = act_ref[...].T
    grad = grad_ref[...]
    for k in range(levels + 1):
        if k < levels:
            field = chosen(fields[k], index_ref, k, block, 0, rows, sub)
            grad_field = chosen(fields[k], index_ref, k, block, rows, rows, sub)
        else:
            field = low_ref[:rows]
            grad_field = low_ref[rows:]
        down = dot(act_t, grad_field).astype(BF)
        up = dot_tn(field, grad).astype(BF)
        for m in range(groups):
            slot = block * groups + m
            group = slot // 3
            row = pl.multiple_of((slot - 3 * group) * piece, piece)
            out_ref[group, k, 0, pl.ds(row, piece), :] = down[m * piece : (m + 1) * piece]
            row = pl.multiple_of(block * piece, piece)
            out_ref[m, k, 1, pl.ds(row, piece), :] = up[m * piece : (m + 1) * piece]


def unpack_kernel(sum_ref, down_ref, left_ref, up_ref, right_ref):
    levels = down_ref.shape[0]
    piece = right_ref.shape[0]
    width = sum_ref.shape[3]
    down_ref[...] = sum_ref[:levels, 0]
    left_ref[...] = sum_ref[levels, 0]
    for b in range(right_ref.shape[1] // width):
        columns = slice(b * width, (b + 1) * width)
        up_ref[:, :, columns] = sum_ref[:levels, 1, b * piece : (b + 1) * piece]
        right_ref[:, columns] = sum_ref[levels, 1, b * piece : (b + 1) * piece]


def late_kernel(groups, both_ref, *refs):
    *pieces, out_ref, low_ref = refs
    assemble(low_ref, pieces)
    rows = low_ref.shape[0] // 2
    right = dot_tn(low_ref[:rows], both_ref[rows:]).astype(BF)
    left = dot_tn(both_ref[:rows], low_ref[rows:]).astype(BF)
    hr = right.shape[0] // groups
    hl = left.shape[0] // groups
    for m in range(groups):
        for c in range(right.shape[1] // 128):
            out_ref[m, c * hr : (c + 1) * hr] = right[m * hr : (m + 1) * hr, c * 128 : (c + 1) * 128]
        base = hr * (right.shape[1] // 128)
        for c in range(left.shape[1] // 128):
            out_ref[m, base + c * hl : base + (c + 1) * hl] = left[
                m * hl : (m + 1) * hl, c * 128 : (c + 1) * 128
            ]


def final_kernel(count, *refs):
    parts = refs[:count]
    low_ref, down_right_ref, up_left_ref, layer_ref, tokens_ref = refs[count:]
    rows = low_ref.shape[0] // 2
    out = dot(low_ref[:rows], down_right_ref[...])
    back = dot_nt(low_ref[rows:], up_left_ref[...])
    for ref in parts:
        out += ref[:rows].astype(F32)
        back += ref[rows:].astype(F32)
    layer_ref[...] = out.astype(BF)
    tokens_ref[...] = back.astype(BF)


def last_kernel(late_ref, right_ref, left_ref):
    late = late_ref[0].astype(F32)
    for m in range(1, late_ref.shape[0]):
        late += late_ref[m].astype(F32)
    late = late.astype(BF)
    hr, hl = right_ref.shape[0], left_ref.shape[0]
    for c in range(right_ref.shape[1] // 128):
        right_ref[:, c * 128 : (c + 1) * 128] = late[c * hr : (c + 1) * hr]
    base = hr * (right_ref.shape[1] // 128)
    for c in range(left_ref.shape[1] // 128):
        left_ref[:, c * 128 : (c + 1) * 128] = late[base + c * hl : base + (c + 1) * hl]


def params():
    return pltpu.CompilerParams(vmem_limit_bytes=VMEM_LIMIT)


def cost(flops, size):
    return pl.CostEstimate(flops=flops, bytes_accessed=size, transcendentals=0)


def group_exchange(pieces, groups):
    return lax.all_to_all(pieces, "hid", 0, 0, axis_index_groups=groups, tiled=True)


def group_scatter(value, groups, beside=None):
    count = len(groups[0])
    pieces = value.reshape(count, value.shape[0] // count, value.shape[1])
    pieces = group_exchange(pieces, groups)
    if beside is not None:
        pieces, beside = lax.optimization_barrier((pieces, beside))
    return jnp.sum(pieces.astype(F32), axis=0).astype(BF), beside


def group_gather(value, groups):
    count = len(groups[0])
    pieces = jnp.broadcast_to(value[None], (count,) + value.shape)
    return group_exchange(pieces, groups).reshape(count * value.shape[0], value.shape[1])


def outer_shift(value, step):
    count, inner = lax.axis_size("hid"), hid_inner()
    return lax.ppermute(value, "hid", [(i, (i + step * inner) % count) for i in range(count)])


def outer_pieces(value):
    return [value] + [outer_shift(value, d) for d in range(1, len(hid_columns()[0]))]


def assemble(out_ref, piece_refs):
    count, tall = len(piece_refs), piece_refs[0].shape[0]
    place = lax.axis_index("hid") // hid_inner()
    for d, ref in enumerate(piece_refs):
        first = pl.multiple_of(lax.rem(place + count - d, count) * tall, tall)
        out_ref[pl.ds(first, tall), :] = ref[...]


def line_step(held, distance):
    count = lax.axis_size("hid")
    other = lax.ppermute(held, "hid", [(i, i ^ distance) for i in range(count)])
    return (held.astype(F32) + other.astype(F32)).astype(BF)


def hid_inner():
    return 8 if lax.axis_size("hid") % 8 == 0 else 1


def hid_columns():
    inner = hid_inner()
    return [list(range(i, lax.axis_size("hid"), inner)) for i in range(inner)]


def in_hbm(value):
    return pltpu.with_memory_space_constraint(value, pltpu.HBM)


def fence(body, *operands):
    shapes = jax.eval_shape(body, *operands)

    def skipped(*_):
        return jax.tree.map(lambda leaf: jnp.zeros(leaf.shape, leaf.dtype), shapes)

    taken = lax.shift_right_logical(lax.axis_index("hid"), 20) == 0
    return lax.cond(taken, body, skipped, *operands)


def line_sum(held, steps):
    def body(value):
        for step in steps:
            value = line_step(value, step)
        return value

    return fence(body, held)


def on_device(
    tokens, cotangent, up_tiles, down_tiles, block_index, up_left, up_right, down_left, down_right
):
    hid_count = lax.axis_size("hid")
    groups = lax.axis_size("tok")
    levels = hid_count.bit_length()
    rows, feat = tokens.shape
    blocks = block_index.shape[1]
    hidden = up_tiles.shape[2]
    width = hidden // blocks
    rank = up_left.shape[1]
    sub = feat // 3
    sds = jax.ShapeDtypeStruct

    def swap(value, distance):
        return lax.ppermute(value, "hid", [(i, i ^ distance) for i in range(hid_count)])

    tie = lax.optimization_barrier
    columns = hid_columns()
    both, low_part = pl.pallas_call(
        head_kernel,
        out_shape=(sds((2 * rows, feat), BF), sds((2 * rows, rank), BF)),
        in_specs=[vmem_spec()] * 4,
        out_specs=(vmem_spec(), vmem_spec()),
        compiler_params=params(),
        cost_estimate=cost(4 * rows * feat * rank, 4 * rows * feat * 2),
        name="head",
    )(tokens, cotangent, up_left, down_right)
    z_two = swap(both, 2)
    total, _ = group_scatter(low_part, columns)
    total, both_x = tie((total, both))
    x_one = swap(both_x, 8)
    x_two = swap(both_x, 16)
    total, z_two, x_one, x_two, both_z = tie(
        (line_sum(total, (6, 1, 2)), z_two, x_one, x_two, both)
    )
    z_four = swap(z_two, 6)
    z_one = swap(both_z, 1)
    low = group_gather(total, columns)
    fields = [both, z_one, z_two, z_four, x_one, x_two]
    part_shapes = [(2 * rows, feat)] * levels

    def whole(shape):
        return pl.BlockSpec(shape, lambda b, *_: (0,) * len(shape))

    grid_params = pltpu.CompilerParams(
        dimension_semantics=("arbitrary",), vmem_limit_bytes=VMEM_LIMIT
    )
    flops = 2 * rows * (levels + 1) * 2 * sub * hidden
    middle = pl.pallas_call(
        functools.partial(middle_kernel, levels),
        grid_spec=pltpu.PrefetchScalarGridSpec(
            num_scalar_prefetch=1,
            grid=(blocks,),
            in_specs=[whole(field.shape) for field in fields]
            + [
                whole((2 * rows, rank)),
                pl.BlockSpec((levels, 2 * sub, width), lambda b, *_: (0, 0, b)),
                pl.BlockSpec((levels, width, 2 * sub), lambda b, *_: (0, b, 0)),
                pl.BlockSpec((rank, width), lambda b, *_: (0, b)),
                pl.BlockSpec((width, rank), lambda b, *_: (b, 0)),
            ],
            out_specs=[
                pl.BlockSpec((rows, width), lambda b, *_: (0, b)),
                pl.BlockSpec((rows, width), lambda b, *_: (0, b)),
                whole((2 * rows, rank)),
            ]
            + [whole(shape) for shape in part_shapes],
            scratch_shapes=[
                pltpu.VMEM((3 * levels, rows, sub), F32),
                pltpu.VMEM((3 * levels, rows, sub), F32),
                pltpu.VMEM((2 * rows, rank), F32),
            ],
        ),
        out_shape=[
            sds((rows, hidden), BF),
            sds((rows, hidden), BF),
            pltpu.HBM((2 * rows, rank), BF),
        ]
        + [pltpu.HBM(shape, BF) for shape in part_shapes],
        compiler_params=grid_params,
        cost_estimate=cost(4 * flops, 10 * 1024 * 1024),
        name="middle",
    )(block_index, *fields, low, *map(in_hbm, (up_tiles, down_tiles, up_right, down_left)))
    act, grad_pre, lowp = middle[:3]
    parts = list(middle[3:])

    piece = width // groups
    packed_shape = (groups, levels + 1, 2, 3 * piece, width)
    grads = pl.pallas_call(
        functools.partial(grads_kernel, levels, groups),
        grid_spec=pltpu.PrefetchScalarGridSpec(
            num_scalar_prefetch=1,
            grid=(blocks,),
            in_specs=[whole(field.shape) for field in fields]
            + [
                whole((2 * rows, rank)),
                pl.BlockSpec((rows, width), lambda b, *_: (0, b)),
                pl.BlockSpec((rows, width), lambda b, *_: (0, b)),
            ],
            out_specs=whole(packed_shape),
        ),
        out_shape=sds(packed_shape, BF),
        compiler_params=grid_params,
        cost_estimate=cost(2 * flops, 10 * 1024 * 1024),
        name="grads",
    )


    own, z_one, z_two, z_four, x_one, x_two = parts
    z_four = swap(z_four, 6)

    packed = grads(block_index, *fields, low, act, grad_pre)
    total, packed = group_scatter(lowp, columns, packed)
    total, z_four, x_one, x_two, z_one = tie(
        (line_sum(total, (2, 1, 6)), z_four, x_one, x_two, z_one)
    )
    z_two = swap((z_two.astype(F32) + z_four.astype(F32)).astype(BF), 2)
    low_pieces = outer_pieces(total)
    x_one = swap(x_one, 8)
    x_two = swap(x_two, 16)
    z_one = swap(z_one, 1)
    summed = lax.psum_scatter(
        packed.reshape(-1, width), "tok", scatter_dimension=0, tiled=True
    ).reshape(packed.shape[1:])
    grad_down_tiles, grad_down_left, grad_up_tiles, grad_up_right = pl.pallas_call(
        unpack_kernel,
        out_shape=(
            sds((levels, hidden // groups, 2 * sub), BF),
            sds((hidden // groups, rank), BF),
            sds((levels, 2 * sub // groups, hidden), BF),
            sds((rank // groups, hidden), BF),
        ),
        in_specs=[vmem_spec()],
        out_specs=(vmem_spec(),) * 4,
        compiler_params=params(),
        cost_estimate=cost(0, packed.size // 2),
        name="unpack",
    )(summed)

    late_rows = (rank // groups) * (feat // 128) + (feat // groups) * (rank // 128)
    late = pl.pallas_call(
        functools.partial(late_kernel, groups),
        out_shape=(sds((groups, late_rows, 128), BF), sds((2 * rows, rank), BF)),
        in_specs=[vmem_spec()] * (1 + len(low_pieces)),
        out_specs=(vmem_spec(),) * 2,
        compiler_params=params(),
        cost_estimate=cost(4 * rows * feat * rank, 4 * rows * feat * 2),
        name="late",
    )

    moved, low2 = late(both, *low_pieces)
    moved = lax.all_to_all(moved, "tok", 0, 0, tiled=True)
    x_two, grad_down_tiles, grad_up_tiles = tie((x_two, grad_down_tiles, grad_up_tiles))
    parts = (own, z_one, z_two, x_one, x_two)
    layer_out, grad_tokens = pl.pallas_call(
        functools.partial(final_kernel, len(parts)),
        out_shape=(sds((rows, feat), BF), sds((rows, feat), BF)),
        in_specs=[vmem_spec()] * (len(parts) + 3),
        out_specs=(vmem_spec(),) * 2,
        compiler_params=params(),
        cost_estimate=cost(4 * rows * feat * rank, 16 * rows * feat * 2),
        name="final",
    )(*parts, low2, down_right, up_left)
    moved, layer_out = tie((moved, layer_out))
    grad_down_right, grad_up_left = pl.pallas_call(
        last_kernel,
        out_shape=(sds((rank // groups, feat), BF), sds((feat // groups, rank), BF)),
        in_specs=[vmem_spec()],
        out_specs=(vmem_spec(),) * 2,
        compiler_params=params(),
        cost_estimate=cost(rows * feat, 3 * rows * feat),
        name="last",
    )(moved)
    return (
        layer_out,
        grad_tokens,
        grad_up_tiles,
        grad_down_tiles,
        grad_up_left,
        grad_up_right,
        grad_down_left,
        grad_down_right,
    )


def solution(mesh):
    return jax.shard_map(
        on_device,
        mesh=mesh,
        in_specs=(
            P("tok", "hid"),
            P("tok", "hid"),
            P(None, None, "hid"),
            P(None, "hid", None),
            P(None, "hid", None),
            P("hid", None),
            P(None, "hid"),
            P("hid", None),
            P(None, "hid"),
        ),
        out_specs=(
            P("tok", "hid"),
            P("tok", "hid"),
            P(None, "tok", "hid"),
            P(None, ("hid", "tok"), None),
            P(("hid", "tok"), None),
            P("tok", "hid"),
            P(("hid", "tok"), None),
            P("tok", "hid"),
        ),
        check_vma=False,
    )
```
